32 devices in a mesh: row: 4 (over z), col: 8 (over y, x, core).
Axes of the slice: x: 2, y: 2, z: 4, core: 2. Of those that a mesh axis runs over, the one named last changes fastest.
Arguments:
- object_field: bfloat16 [2, 2048, 4096], P(None, 'row', 'col'), may hold values from -6 to 6
- probe_modes: float32 [2, 2, 256, 256], replicated, may hold values from -6 to 6
- measured_amp: bfloat16 [4, 8, 8, 256, 256], P('row', 'col'), may hold values from 0.25 to 8
- scan_positions: int32 [4, 8, 2, 8], P('row', 'col'), may hold values from 0 to 512
- frame_counts: int32 [4, 8], P('row', 'col'), may hold values from 1 to 8, as said below
Outputs:
- object_grad: float32 [2, 2048, 4096], P(None, 'row', 'col')
- probe_grad: float32 [2, 2, 256, 256], replicated
The draws below stay inside these ranges and needn't reach their ends.
Inputs may be any that keep to these rules, and one draw needn't show every extreme that they name: `frame_counts`: live frames of a tile; slots at or past it are ignored; some tile has exactly 8.
All inputs are finite; a program needn't handle non-finite values.
Results may differ from the reference program's by a relative error of at most 0.0059.
The reference program's roundings to bfloat16 on the way count: a program that leaves them out, or rounds other values in their place, can miss the bound.
Values may be sent and summed in bfloat16 or wider, within the bound.
A program may use at most 64 MiB of HBM per device.

```python
import math
import jax
import jax.numpy as jnp
from jax import lax

FS = 256
MODES = 2
TILE = 512
HALO = 128
FR_MAX = 8
NR = 2048
NC = 4096
N_ROW = 4
N_COL = 8


def draw_frame_counts(key, part):
    first_key = jax.random.fold_in(key, 11)
    second_key = jax.random.fold_in(key, 12)
    third_key = jax.random.fold_in(key, 13)
    base_counts = jax.random.randint(first_key, (N_ROW * N_COL,), FR_MAX // 4 + 1, 3 * FR_MAX // 4 + 1)
    heavy = jax.random.randint(second_key, (N_ROW * N_COL,), 0, 4) == 0
    chosen = jax.random.randint(third_key, (), 0, N_ROW * N_COL)
    places = jnp.arange(N_ROW * N_COL, dtype=jnp.int32)
    counts_flat = jnp.where(heavy | (places == chosen), FR_MAX, base_counts)
    return counts_flat.reshape(N_ROW, N_COL).astype(jnp.int32)


def place_ends(drawn, rng, least, high):
    shape = drawn.shape
    place = [jax.random.randint(jax.random.fold_in(rng, axis), (), 0, shape[axis]) for axis in range(len(shape))]
    drawn = drawn.at[tuple(place)].set(least)
    longest = shape.index(max(shape))
    place[longest] = (place[longest] + 1) % shape[longest]
    return drawn.at[tuple(place)].set(high)


def block_levels(own_key, dims, split, least, top_value):
    gain, own = 1.0, jax.random.fold_in(own_key, 6)
    for dim, parts in split:
        heights = jnp.exp(jax.random.uniform(jax.random.fold_in(own, dim), (parts,), jnp.float32, least / len(split), top_value / len(split)))
        gain = gain * jnp.repeat(heights, dims[dim] // parts).reshape([-1 if axis == dim else 1 for axis in range(len(dims))])
    return gain


def scatter_about(key, shape, width, bound, cuts=(), held_as=jnp.bfloat16):
    gain = block_levels(key, shape, cuts, -0.22, 0.18) if cuts else 1.0
    entries = jax.random.normal(key, shape, jnp.float32) * width * gain
    return jnp.minimum(jnp.maximum(entries, -bound), bound).astype(held_as)


def setup_inputs(seed: int = 0) -> dict:
    seeds = jax.random.split(jax.random.key(seed), 6)
    object_field = scatter_about(seeds[0], (2, NR, NC), 1.0, 6.0, ((1, 4), (2, 8)))
    probe_modes = scatter_about(seeds[1], (2, MODES, FS, FS), 1.0, 6.0, (), jnp.float32)
    measured_amp = jnp.clip(jnp.exp(math.log(8.0) - 3.465736 * jax.random.uniform(seeds[2], (N_ROW, N_COL, FR_MAX, FS, FS), jnp.float32) ** block_levels(seeds[2], (N_ROW, N_COL, FR_MAX, FS, FS), ((0, 4), (1, 8)), -0.2, 0.2)), 0.25, 8.0).astype(jnp.bfloat16)
    scan_positions = place_ends(jax.random.randint(seeds[3], (N_ROW, N_COL, 2, FR_MAX), 0, TILE + 2 * HALO - FS + 1), jax.random.fold_in(seeds[3], 1), 0, TILE + 2 * HALO - FS).astype(jnp.int32)
    frame_counts = draw_frame_counts(jax.random.fold_in(seeds[5], 71), 0)
    return {"object_field": object_field, "probe_modes": probe_modes, "measured_amp": measured_amp, "scan_positions": scan_positions, "frame_counts": frame_counts}


def fourier_tables(frame_side):
    indices = jnp.arange(frame_side, dtype=jnp.int32)
    product = indices[:, None] * indices[None, :] % frame_side
    angles = 2.0 * math.pi / frame_side * product.astype(jnp.float32)
    norm_scale = 1.0 / math.sqrt(frame_side)
    return ((jnp.cos(angles) * norm_scale).astype(jnp.bfloat16), (-jnp.sin(angles) * norm_scale).astype(jnp.bfloat16))

def left_mul(table, data):
    return jnp.einsum('kn,mnj->mkj', table.astype(jnp.float32), data.astype(jnp.float32))

def right_mul(data, table):
    return jnp.einsum('mkn,nj->mkj', data.astype(jnp.float32), table.astype(jnp.float32))

def transform(real_part, imag_part, table_real, table_imag):
    first_real = (left_mul(table_real, real_part) - left_mul(table_imag, imag_part)).astype(jnp.bfloat16)
    first_imag = (left_mul(table_real, imag_part) + left_mul(table_imag, real_part)).astype(jnp.bfloat16)
    out_real = right_mul(first_real, table_real) - right_mul(first_imag, table_imag)
    out_imag = right_mul(first_real, table_imag) + right_mul(first_imag, table_real)
    return (out_real, out_imag)

def frame_terms(frame_patch, frame_amp, probe_modes, table_real, table_imag):
    probe_real = probe_modes[0]
    probe_imag = probe_modes[1]
    patch_real = frame_patch[0].astype(jnp.float32)
    patch_imag = frame_patch[1].astype(jnp.float32)
    exit_real = (probe_real * patch_real - probe_imag * patch_imag).astype(jnp.bfloat16)
    exit_imag = (probe_real * patch_imag + probe_imag * patch_real).astype(jnp.bfloat16)
    psi_real, psi_imag = transform(exit_real, exit_imag, table_real, table_imag)
    power = lax.optimization_barrier(jnp.sum(psi_real * psi_real + psi_imag * psi_imag, axis=0))
    factor = 1.0 - frame_amp.astype(jnp.float32) / jnp.maximum(jnp.sqrt(power), 0.5)
    chi_real = (psi_real * factor).astype(jnp.bfloat16)
    chi_imag = (psi_imag * factor).astype(jnp.bfloat16)
    back_real, back_imag = transform(chi_real, chi_imag, table_real, -table_imag)
    patch_grad = jnp.stack([lax.optimization_barrier(jnp.sum(probe_real * back_real + probe_imag * back_imag, axis=0)), lax.optimization_barrier(jnp.sum(probe_real * back_imag - probe_imag * back_real, axis=0))])
    probe_term = jnp.stack([patch_real * back_real + patch_imag * back_imag, patch_real * back_imag - patch_imag * back_real])
    return (patch_grad, probe_term)

def reference(object_field, probe_modes, measured_amp, scan_positions, frame_counts):
    table_real, table_imag = fourier_tables(FS)
    padded = jnp.pad(object_field, ((0, 0), (HALO, HALO), (HALO, HALO)))
    start_pair = (jnp.zeros(padded.shape, jnp.float32), jnp.zeros(probe_modes.shape, jnp.float32))

    def visit(position, state_pair):
        position = jnp.asarray(position).astype(jnp.int32)
        tile_row = position // (N_COL * FR_MAX)
        tile_col = position // FR_MAX % N_COL
        slot_at = position % FR_MAX

        def advance(inner_pair):
            gradient, probe_total = inner_pair
            row_at = (tile_row * TILE + scan_positions[tile_row, tile_col, 0, slot_at]).astype(jnp.int32)
            column_at = (tile_col * TILE + scan_positions[tile_row, tile_col, 1, slot_at]).astype(jnp.int32)
            zero_index = jnp.zeros((), jnp.int32)
            frame_patch = lax.dynamic_slice(padded, (zero_index, row_at, column_at), (2, FS, FS))
            patch_grad, probe_term = frame_terms(frame_patch, measured_amp[tile_row, tile_col, slot_at], probe_modes, table_real, table_imag)
            old_block = lax.dynamic_slice(gradient, (zero_index, row_at, column_at), (2, FS, FS))
            gradient = lax.dynamic_update_slice(gradient, old_block + patch_grad, (zero_index, row_at, column_at))
            return (gradient, probe_total + probe_term)
        return lax.cond(slot_at < frame_counts[tile_row, tile_col], advance, lambda unchanged: unchanged, state_pair)
    gradient, probe_total = lax.fori_loop(0, N_ROW * N_COL * FR_MAX, visit, start_pair)
    norm_scale = 1.0 / math.sqrt(N_ROW * N_COL * FR_MAX)
    return (gradient[:, HALO:HALO + N_ROW * TILE, HALO:HALO + N_COL * TILE], probe_total * norm_scale)
```

```python
import math

import jax
import jax.numpy as jnp
from jax import lax
from jax.experimental import pallas as pl
from jax.experimental.pallas import tpu as pltpu
from jax.sharding import PartitionSpec as P

HALO = 128


def with_halo(value, sides, width):
    for axis, dim in sides:
        devices, length = (lax.axis_size(axis), value.shape[dim])
        up = [(i, (i + 1) % devices) for i in range(devices - 1)]
        down = [(j, i) for i, j in up]
        last = lax.slice_in_dim(value, length - width, length, axis=dim)
        leading = lax.slice_in_dim(value, 0, width, axis=dim)
        before = lax.ppermute(last, axis, up)
        after = lax.ppermute(leading, axis, down)
        value = jnp.concatenate([before, value, after], axis=dim)
    return value


def from_behind(value, axis, by):
    devices = lax.axis_size(axis)
    pairs = [(i, i + by) for i in range(devices) if 0 <= i + by < devices]
    return lax.ppermute(value, axis, pairs)


def fourier_tables(frame_side):
    indices = jnp.arange(frame_side, dtype=jnp.int32)
    product = indices[:, None] * indices[None, :] % frame_side
    angles = 2.0 * math.pi / frame_side * product.astype(jnp.float32)
    norm_scale = 1.0 / math.sqrt(frame_side)
    return (
        (jnp.cos(angles) * norm_scale).astype(jnp.bfloat16),
        (-jnp.sin(angles) * norm_scale).astype(jnp.bfloat16),
    )


LANES = 128
CHUNK = 32


def dot32(left, right):
    return jnp.dot(left, right, preferred_element_type=jnp.float32)


def frames_kernel(
    count_ref, at_ref, ext_ref, probe_ref, amp_ref, tr_ref, ti_ref, acc_ref, pacc_ref,
    extf, fwd, inv, stage, half, wide, patch,
):
    fs = probe_ref.shape[-1]
    modes = probe_ref.shape[1]
    tiles = ext_ref.shape[2] // LANES
    lane_tiles = fs // LANES
    for plane in range(2):
        for t in range(tiles):
            extf[plane, t] = ext_ref[plane, :, t * LANES : (t + 1) * LANES].astype(jnp.float32)
        extf[plane, tiles] = jnp.zeros(extf.shape[2:], jnp.float32)
    acc_ref[...] = jnp.zeros(acc_ref.shape, jnp.float32)
    pacc_ref[...] = jnp.zeros(pacc_ref.shape, jnp.float32)
    table_real, table_imag = tr_ref[...], ti_ref[...]
    minus = -table_imag
    fwd[:fs, :fs] = table_real
    fwd[:fs, fs:] = minus
    fwd[fs:, :fs] = table_imag
    fwd[fs:, fs:] = table_real
    inv[:fs, :fs] = table_real
    inv[:fs, fs:] = table_imag
    inv[fs:, :fs] = minus
    inv[fs:, fs:] = table_real

    def two_sided(left_table, right_table):
        for m in range(modes):
            both = dot32(left_table[...], stage[:, m * fs : (m + 1) * fs])
            half[m * fs : (m + 1) * fs, :fs] = both[:fs].astype(jnp.bfloat16)
            half[m * fs : (m + 1) * fs, fs:] = both[fs:].astype(jnp.bfloat16)
        wide[...] = dot32(half[...], right_table[...])

    def advance(slot, carry):
        row_at = at_ref[0, slot]
        col_at = at_ref[1, slot]
        tile_at = col_at // LANES
        shift = col_at % LANES
        back_shift = (LANES - shift) % LANES
        lane = lax.broadcasted_iota(jnp.int32, (CHUNK, LANES), 1)
        keep_low = lane < LANES - shift
        from_same = lane >= shift
        for r in range(0, fs, CHUNK):
            rows = slice(r, r + CHUNK)
            values = []
            for plane in range(2):
                rolled = [
                    pltpu.roll(
                        extf[plane, tile_at + t, pl.ds(row_at + r, CHUNK), :], back_shift, 1
                    )
                    for t in range(lane_tiles + 1)
                ]
                values.append(
                    [jnp.where(keep_low, rolled[t], rolled[t + 1]) for t in range(lane_tiles)]
                )
            for t in range(lane_tiles):
                cols = slice(t * LANES, (t + 1) * LANES)
                patch_real, patch_imag = values[0][t], values[1][t]
                patch[0, rows, cols] = patch_real
                patch[1, rows, cols] = patch_imag
                for m in range(modes):
                    probe_real = probe_ref[0, m, rows, cols]
                    probe_imag = probe_ref[1, m, rows, cols]
                    out = slice(m * fs + t * LANES, m * fs + (t + 1) * LANES)
                    stage[rows, out] = (
                        probe_real * patch_real - probe_imag * patch_imag
                    ).astype(jnp.bfloat16)
                    stage[fs + r : fs + r + CHUNK, out] = (
                        probe_real * patch_imag + probe_imag * patch_real
                    ).astype(jnp.bfloat16)
        two_sided(fwd, inv)
        for r in range(0, fs, CHUNK):
            for t in range(lane_tiles):
                cols = slice(t * LANES, (t + 1) * LANES)
                imag_cols = slice(fs + t * LANES, fs + (t + 1) * LANES)
                psi = []
                power = jnp.zeros((CHUNK, LANES), jnp.float32)
                for m in range(modes):
                    rows = slice(m * fs + r, m * fs + r + CHUNK)
                    real, imag = wide[rows, cols], wide[rows, imag_cols]
                    psi.append((real, imag))
                    power = power + (real * real + imag * imag)
                amp = amp_ref[slot, r : r + CHUNK, cols].astype(jnp.float32)
                factor = 1.0 - amp * lax.rsqrt(jnp.maximum(power, 0.25))
                for m in range(modes):
                    out = slice(m * fs + t * LANES, m * fs + (t + 1) * LANES)
                    stage[r : r + CHUNK, out] = (psi[m][0] * factor).astype(jnp.bfloat16)
                    stage[fs + r : fs + r + CHUNK, out] = (psi[m][1] * factor).astype(jnp.bfloat16)
        two_sided(inv, fwd)
        for r in range(0, fs, CHUNK):
            grads = [[], []]
            for t in range(lane_tiles):
                cols = slice(t * LANES, (t + 1) * LANES)
                imag_cols = slice(fs + t * LANES, fs + (t + 1) * LANES)
                patch_real = patch[0, r : r + CHUNK, cols]
                patch_imag = patch[1, r : r + CHUNK, cols]
                total_real = total_imag = 0.0
                for m in range(modes):
                    rows = slice(m * fs + r, m * fs + r + CHUNK)
                    real, imag = wide[rows, cols], wide[rows, imag_cols]
                    probe_real = probe_ref[0, m, r : r + CHUNK, cols]
                    probe_imag = probe_ref[1, m, r : r + CHUNK, cols]
                    total_real = total_real + (probe_real * real + probe_imag * imag)
                    total_imag = total_imag + (probe_real * imag - probe_imag * real)
                    at = (m * lane_tiles + t) * fs + r
                    pacc_ref[at : at + CHUNK, :] += patch_real * real + patch_imag * imag
                    at += modes * lane_tiles * fs
                    pacc_ref[at : at + CHUNK, :] += patch_real * imag - patch_imag * real
                grads[0].append(pltpu.roll(total_real, shift, 1))
                grads[1].append(pltpu.roll(total_imag, shift, 1))
            for plane in range(2):
                rolled = grads[plane]
                for t in range(lane_tiles + 1):
                    same = rolled[t] if t < lane_tiles else 0.0
                    before = rolled[t - 1] if t > 0 else 0.0
                    where = (plane, tile_at + t, pl.ds(row_at + r, CHUNK), slice(None))
                    acc_ref[where] += jnp.where(from_same, same, before)
        return carry

    lax.fori_loop(0, count_ref[0], advance, 0)


def frames_call(extended, probe_modes, amplitudes, positions, live_count, tables):
    fs = probe_modes.shape[-1]
    modes = probe_modes.shape[1]
    ext_rows, ext_cols = extended.shape[1:]
    tiled = (2, ext_cols // LANES + 1, ext_rows, LANES)
    vmem = pl.BlockSpec(memory_space=pltpu.VMEM)
    smem = pl.BlockSpec(memory_space=pltpu.SMEM)
    return pl.pallas_call(
        frames_kernel,
        out_shape=(
            jax.ShapeDtypeStruct(tiled, jnp.float32),
            jax.ShapeDtypeStruct((probe_modes.size // LANES, LANES), jnp.float32),
        ),
        in_specs=[smem, smem, vmem, vmem, vmem, vmem, vmem],
        out_specs=(vmem, vmem),
        scratch_shapes=[
            pltpu.VMEM(tiled, jnp.float32),
            pltpu.VMEM((2 * fs, 2 * fs), jnp.bfloat16),
            pltpu.VMEM((2 * fs, 2 * fs), jnp.bfloat16),
            pltpu.VMEM((2 * fs, modes * fs), jnp.bfloat16),
            pltpu.VMEM((modes * fs, 2 * fs), jnp.bfloat16),
            pltpu.VMEM((modes * fs, 2 * fs), jnp.float32),
            pltpu.VMEM((2, fs, fs), jnp.float32),
        ],
        compiler_params=pltpu.CompilerParams(vmem_limit_bytes=56 * 1024 * 1024),
        name="frames",
    )(live_count.reshape(1), positions, extended, probe_modes, amplitudes, *tables)


def shards(object_field, probe_modes, measured_amp, scan_positions, frame_counts):
    frame_side = probe_modes.shape[-1]
    slot_count = measured_amp.shape[2]
    tile_side = object_field.shape[1]
    extended = with_halo(object_field, (("row", 1), ("col", 2)), HALO)
    amplitudes = measured_amp[0, 0]
    acc, probe_flat = frames_call(
        extended,
        probe_modes,
        amplitudes,
        scan_positions[0, 0],
        frame_counts[0, 0],
        fourier_tables(frame_side),
    )
    gradient = acc[:, :-1].transpose(0, 2, 1, 3).reshape(extended.shape)
    modes = probe_modes.shape[1]
    probe_local = probe_flat.reshape(2, modes, frame_side // LANES, frame_side, LANES)
    probe_local = probe_local.transpose(0, 1, 3, 2, 4).reshape(probe_modes.shape)
    low_end = tile_side + HALO
    from_above = from_behind(gradient[:, low_end:, :].astype(jnp.bfloat16), "row", 1).astype(
        jnp.float32
    )
    from_below = from_behind(gradient[:, :HALO, :].astype(jnp.bfloat16), "row", -1).astype(
        jnp.float32
    )
    middle = gradient[:, HALO:low_end, :]
    middle = middle.at[:, :HALO, :].add(from_above)
    middle = middle.at[:, tile_side - HALO :, :].add(from_below)
    from_left = from_behind(middle[:, :, low_end:].astype(jnp.bfloat16), "col", 1).astype(
        jnp.float32
    )
    from_right = from_behind(middle[:, :, :HALO].astype(jnp.bfloat16), "col", -1).astype(
        jnp.float32
    )
    interior = middle[:, :, HALO:low_end]
    interior = interior.at[:, :, :HALO].add(from_left)
    interior = interior.at[:, :, tile_side - HALO :].add(from_right)
    probe_total = lax.psum(probe_local, ("row", "col"))
    norm_scale = 1.0 / math.sqrt(lax.axis_size("row") * lax.axis_size("col") * slot_count)
    return (interior, probe_total * norm_scale)


def solution(mesh):
    in_specs = (
        P(None, "row", "col"),
        P(),
        P("row", "col", None, None, None),
        P("row", "col", None, None),
        P("row", "col"),
    )
    out_specs = (P(None, "row", "col"), P())
    return jax.shard_map(shards, mesh=mesh, in_specs=in_specs, out_specs=out_specs, check_vma=False)
```

```python
import functools
import math

import jax
import jax.numpy as jnp
import numpy as np
from jax import lax
from jax.experimental import pallas as pl
from jax.experimental.pallas import tpu as pltpu
from jax.sharding import PartitionSpec as P

HALO = 128
LANES = 128


MESH = pl.DeviceIdType.MESH
SIDES = [(dr, dc) for dr in (-1, 0, 1) for dc in (-1, 0, 1) if (dr, dc) != (0, 0)]


def position():
    return (
        lax.axis_index("row"),
        lax.axis_index("col"),
        lax.axis_size("row"),
        lax.axis_size("col"),
    )


def exists(side):
    row, col, rows, cols = position()
    dr, dc = side
    inside = jnp.bool_(True)
    if dr:
        inside = row + dr >= 0 if dr < 0 else row + dr < rows
    if dc:
        other = col + dc >= 0 if dc < 0 else col + dc < cols
        inside = jnp.logical_and(inside, other) if dr else other
    return inside


def at_side(side):
    row, col, _, _ = position()
    return (row + side[0], col + side[1])


def opposite(side):
    return (-side[0], -side[1])


def part(step, margin, inner):
    return {-1: slice(0, margin), 0: slice(margin, margin + inner), 1: slice(margin + inner, None)}[
        step
    ]


def edge(step, margin, inner):
    return {-1: slice(0, margin), 0: slice(0, inner), 1: slice(inner - margin, inner)}[step]


def to_side(side, index, source, landing, send_sems, recv_sems):
    return pltpu.make_async_remote_copy(
        src_ref=source,
        dst_ref=landing,
        send_sem=send_sems.at[index],
        recv_sem=recv_sems.at[index],
        device_id=at_side(side),
        device_id_type=MESH,
    )


def halo_kernel(object_ref, ext_ref, *scratch):
    landings, (send_sems, recv_sems) = scratch[: len(SIDES)], scratch[len(SIDES) :]
    side_rows, side_cols = object_ref.shape[1:]
    barrier = pltpu.get_barrier_semaphore()
    count = jnp.int32(0)
    for side in SIDES:

        @pl.when(exists(side))
        def _(side=side):
            pl.semaphore_signal(barrier, inc=1, device_id=at_side(side), device_id_type=MESH)

        count = count + exists(side).astype(jnp.int32)
    pl.semaphore_wait(barrier, count)

    def copy(index):
        dr, dc = SIDES[index]
        source = object_ref.at[:, edge(dr, HALO, side_rows), edge(dc, HALO, side_cols)]
        return to_side(SIDES[index], index, source, landings[index], send_sems, recv_sems)

    for index, side in enumerate(SIDES):

        @pl.when(exists(side))
        def _(index=index):
            copy(index).start()

    for t in range(side_cols // LANES):
        ext_ref[:, HALO // LANES + t, HALO : HALO + side_rows, :] = object_ref[
            :, :, t * LANES : (t + 1) * LANES
        ]
    for index, side in enumerate(SIDES):
        dr, dc = opposite(side)
        rows = part(dr, HALO, side_rows)
        tiles = range(ext_ref.shape[1])[part(dc, HALO // LANES, side_cols // LANES)]

        @pl.when(exists((dr, dc)))
        def _(index=index, rows=rows, tiles=tiles):
            copy(index).wait_recv()
            for k, t in enumerate(tiles):
                ext_ref[:, t, rows, :] = landings[index][:, :, k * LANES : (k + 1) * LANES]

        @pl.when(jnp.logical_not(exists((dr, dc))))
        def _(rows=rows, tiles=tiles, index=index):
            for t in tiles:
                ext_ref[:, t, rows, :] = jnp.zeros(
                    (2, landings[index].shape[1], LANES), ext_ref.dtype
                )

    for index, side in enumerate(SIDES):

        @pl.when(exists(side))
        def _(index=index):
            copy(index).wait_send()


def halo_call(object_field):
    _, side_rows, side_cols = object_field.shape
    vmem = pl.BlockSpec(memory_space=pltpu.VMEM)
    landings = []
    for dr, dc in SIDES:
        landings.append(
            pltpu.VMEM((2, HALO if dr else side_rows, HALO if dc else side_cols), object_field.dtype)
        )
    sems = pltpu.SemaphoreType.DMA((len(SIDES),))
    return pl.pallas_call(
        halo_kernel,
        out_shape=jax.ShapeDtypeStruct(
            (2, (side_cols + 2 * HALO) // LANES, side_rows + 2 * HALO, LANES), object_field.dtype
        ),
        in_specs=[vmem],
        out_specs=vmem,
        scratch_shapes=landings + [sems, sems],
        compiler_params=pltpu.CompilerParams(
            collective_id=0, has_side_effects=True, vmem_limit_bytes=32 * 1024 * 1024
        ),
        name="halo",
    )(object_field)


def reduce_kernel(scale, acc_ref, pacc_ref, grad_ref, probe_ref, *scratch):
    count = len(SIDES)
    sends, landings, rest = scratch[:count], scratch[count : 2 * count], scratch[2 * count :]
    psend, precv, zsend, zrecv, full, side_sems, col_sems, row_sems = rest
    row, col, n_row, n_col = position()
    side_rows, side_cols = grad_ref.shape[1:]
    margin = HALO // LANES
    inner = side_cols // LANES
    for index, (dr, dc) in enumerate(SIDES):
        tiles = range(inner + 2 * margin)[part(dc, margin, inner)]
        rows = part(dr, HALO, side_rows)
        for k, t in enumerate(tiles):
            sends[index][:, k] = acc_ref[:, t, rows, :].astype(jnp.bfloat16)
    psend[...] = pacc_ref[...].astype(jnp.bfloat16)

    barrier = pltpu.get_barrier_semaphore()
    waits = jnp.int32(n_row + n_col - 2)
    for k in range(1, n_col):
        pl.semaphore_signal(
            barrier, inc=1, device_id=(row, lax.rem(col + k, n_col)), device_id_type=MESH
        )
    for k in range(1, n_row):
        pl.semaphore_signal(
            barrier, inc=1, device_id=(lax.rem(row + k, n_row), col), device_id_type=MESH
        )
    for side in SIDES:
        if side[0] and side[1]:

            @pl.when(exists(side))
            def _(side=side):
                pl.semaphore_signal(barrier, inc=1, device_id=at_side(side), device_id_type=MESH)

            waits = waits + exists(side).astype(jnp.int32)
    pl.semaphore_wait(barrier, waits)

    share = psend.shape[0] // n_col
    piece = share // n_row

    def to_peer(source, landing, sems, which, k, device):
        return pltpu.make_async_remote_copy(
            src_ref=source,
            dst_ref=landing,
            send_sem=sems.at[which, k - 1],
            recv_sem=sems.at[which + 1, k - 1],
            device_id=device,
            device_id_type=MESH,
        )

    def col_peer(k):
        return (row, lax.rem(col + k, n_col))

    def row_peer(k):
        return (lax.rem(row + k, n_row), col)

    def share_of(ref, index):
        return ref.at[pl.ds(pl.multiple_of(index * share, share), share)]

    def scatter_copy(k):
        return to_peer(
            share_of(psend, lax.rem(col + k, n_col)), precv.at[k - 1], col_sems, 0, k, col_peer(k)
        )

    def row_scatter_copy(k):
        target = lax.rem(row + k, n_row)
        return to_peer(
            zsend.at[pl.ds(pl.multiple_of(target * piece, piece), piece)],
            zrecv.at[k - 1],
            row_sems,
            0,
            k,
            row_peer(k),
        )

    def piece_of(index):
        start = pl.multiple_of(col * share + index * piece, piece)
        return full.at[pl.ds(start, piece)]

    def row_gather_copy(k, owner):
        return to_peer(piece_of(row), piece_of(owner), row_sems, 2, k, row_peer(k))

    def gather_copy(k, owner):
        return to_peer(share_of(full, col), share_of(full, owner), col_sems, 2, k, col_peer(k))

    def side_copy(index):
        return to_side(
            SIDES[index], index, sends[index], landings[index], side_sems.at[0], side_sems.at[1]
        )

    for k in range(1, n_col):
        scatter_copy(k).start()
    for index, side in enumerate(SIDES):

        @pl.when(exists(side))
        def _(index=index):
            side_copy(index).start()

    for t in range(inner):
        grad_ref[:, :, t * LANES : (t + 1) * LANES] = acc_ref[
            :, margin + t, HALO : HALO + side_rows, :
        ]
    total = pacc_ref[pl.ds(pl.multiple_of(col * share, share), share), :]
    for k in range(1, n_col):
        scatter_copy(k).wait_recv()
        total = total + precv[k - 1].astype(jnp.float32)
    zsend[...] = total
    for k in range(1, n_row):
        row_scatter_copy(k).start()
    own = zsend[pl.ds(pl.multiple_of(row * piece, piece), piece), :]
    for k in range(1, n_row):
        row_scatter_copy(k).wait_recv()
        own = own + zrecv[k - 1]
    start = pl.multiple_of(col * share + row * piece, piece)
    full[pl.ds(start, piece), :] = (own * scale).astype(jnp.bfloat16)
    for k in range(1, n_row):
        row_gather_copy(k, row).start()
    for k in range(1, n_row):
        row_gather_copy(k, lax.rem(row + n_row - k, n_row)).wait_recv()
    for k in range(1, n_col):
        gather_copy(k, col).start()

    for index, side in enumerate(SIDES):
        dr, dc = opposite(side)
        rows = edge(dr, HALO, side_rows)
        tiles = range(inner)[edge(dc, margin, inner)]

        @pl.when(exists((dr, dc)))
        def _(index=index, rows=rows, tiles=tiles):
            side_copy(index).wait_recv()
            for k, t in enumerate(tiles):
                grad_ref[:, rows, t * LANES : (t + 1) * LANES] += landings[index][:, k].astype(
                    jnp.float32
                )

    for k in range(1, n_col):
        gather_copy(k, lax.rem(col + n_col - k, n_col)).wait_recv()
    parts, modes, fs, width = probe_ref.shape
    at = 0
    for p in range(parts):
        for m in range(modes):
            for t in range(width // LANES):
                probe_ref[p, m, :, t * LANES : (t + 1) * LANES] = full[at : at + fs, :].astype(
                    jnp.float32
                )
                at += fs
    for k in range(1, n_col):
        scatter_copy(k).wait_send()
        gather_copy(k, col).wait_send()
    for k in range(1, n_row):
        row_scatter_copy(k).wait_send()
        row_gather_copy(k, row).wait_send()
    for index, side in enumerate(SIDES):

        @pl.when(exists(side))
        def _(index=index):
            side_copy(index).wait_send()


def reduce_call(acc, probe_flat, object_shape, probe_shape, scale):
    n_row, n_col = lax.axis_size("row"), lax.axis_size("col")
    _, side_rows, side_cols = object_shape
    inner = side_cols // LANES
    margin = HALO // LANES
    vmem = pl.BlockSpec(memory_space=pltpu.VMEM)
    buffers = []
    for dr, dc in SIDES:
        buffers.append(
            pltpu.VMEM(
                (2, margin if dc else inner, HALO if dr else side_rows, LANES), jnp.bfloat16
            )
        )
    total_rows = probe_flat.shape[0]
    share = total_rows // n_col
    piece = share // n_row
    return pl.pallas_call(
        functools.partial(reduce_kernel, scale),
        out_shape=(
            jax.ShapeDtypeStruct(object_shape, jnp.float32),
            jax.ShapeDtypeStruct(probe_shape, jnp.float32),
        ),
        in_specs=[vmem, vmem],
        out_specs=(vmem, vmem),
        scratch_shapes=buffers
        + buffers
        + [
            pltpu.VMEM((total_rows, LANES), jnp.bfloat16),
            pltpu.VMEM((n_col - 1, share, LANES), jnp.bfloat16),
            pltpu.VMEM((share, LANES), jnp.float32),
            pltpu.VMEM((n_row - 1, piece, LANES), jnp.float32),
            pltpu.VMEM((total_rows, LANES), jnp.bfloat16),
            pltpu.SemaphoreType.DMA((2, len(SIDES))),
            pltpu.SemaphoreType.DMA((4, n_col - 1)),
            pltpu.SemaphoreType.DMA((4, n_row - 1)),
        ],
        compiler_params=pltpu.CompilerParams(
            collective_id=1, has_side_effects=True, vmem_limit_bytes=48 * 1024 * 1024
        ),
        name="reduce",
    )(acc, probe_flat)


def fourier_tables(frame_side):
    indices = np.arange(frame_side)
    product = indices[:, None] * indices[None, :] % frame_side
    angles = 2.0 * math.pi / frame_side * product
    norm_scale = 1.0 / math.sqrt(frame_side)
    return (
        jnp.asarray((np.cos(angles) * norm_scale).astype(np.float32)).astype(jnp.bfloat16),
        jnp.asarray((-np.sin(angles) * norm_scale).astype(np.float32)).astype(jnp.bfloat16),
    )


CHUNK = 32


def dot32(left, right):
    return jnp.dot(left, right, preferred_element_type=jnp.float32)


def frames_kernel(
    count_ref, at_ref, ext_ref, probe_ref, amp_ref, tr_ref, ti_ref, acc_ref, pacc_ref,
    extf, fwd, inv, stage, half, wide, patch,
):
    fs = probe_ref.shape[-1]
    modes = probe_ref.shape[1]
    tiles = ext_ref.shape[1]
    lane_tiles = fs // LANES
    for plane in range(2):
        for t in range(tiles):
            extf[plane, t] = ext_ref[plane, t].astype(jnp.float32)
        extf[plane, tiles] = jnp.zeros(extf.shape[2:], jnp.float32)
    acc_ref[...] = jnp.zeros(acc_ref.shape, jnp.float32)
    pacc_ref[...] = jnp.zeros(pacc_ref.shape, jnp.float32)
    table_real, table_imag = tr_ref[...], ti_ref[...]
    minus = -table_imag
    fwd[:fs, :fs] = table_real
    fwd[:fs, fs:] = minus
    fwd[fs:, :fs] = table_imag
    fwd[fs:, fs:] = table_real
    inv[:fs, :fs] = table_real
    inv[:fs, fs:] = table_imag
    inv[fs:, :fs] = minus
    inv[fs:, fs:] = table_real

    def two_sided(left_table, right_table):
        for m in range(modes):
            both = dot32(left_table[...], stage[:, m * fs : (m + 1) * fs])
            half[m * fs : (m + 1) * fs, :fs] = both[:fs].astype(jnp.bfloat16)
            half[m * fs : (m + 1) * fs, fs:] = both[fs:].astype(jnp.bfloat16)
        wide[...] = dot32(half[...], right_table[...])

    def advance(slot, carry):
        row_at = at_ref[0, slot]
        col_at = at_ref[1, slot]
        tile_at = col_at // LANES
        shift = col_at % LANES
        back_shift = (LANES - shift) % LANES
        lane = lax.broadcasted_iota(jnp.int32, (CHUNK, LANES), 1)
        keep_low = lane < LANES - shift
        from_same = lane >= shift
        for r in range(0, fs, CHUNK):
            rows = slice(r, r + CHUNK)
            values = []
            for plane in range(2):
                rolled = [
                    pltpu.roll(
                        extf[plane, tile_at + t, pl.ds(row_at + r, CHUNK), :], back_shift, 1
                    )
                    for t in range(lane_tiles + 1)
                ]
                values.append(
                    [jnp.where(keep_low, rolled[t], rolled[t + 1]) for t in range(lane_tiles)]
                )
            for t in range(lane_tiles):
                cols = slice(t * LANES, (t + 1) * LANES)
                patch_real, patch_imag = values[0][t], values[1][t]
                patch[0, rows, cols] = patch_real
                patch[1, rows, cols] = patch_imag
                for m in range(modes):
                    probe_real = probe_ref[0, m, rows, cols]
                    probe_imag = probe_ref[1, m, rows, cols]
                    out = slice(m * fs + t * LANES, m * fs + (t + 1) * LANES)
                    stage[rows, out] = (
                        probe_real * patch_real - probe_imag * patch_imag
                    ).astype(jnp.bfloat16)
                    stage[fs + r : fs + r + CHUNK, out] = (
                        probe_real * patch_imag + probe_imag * patch_real
                    ).astype(jnp.bfloat16)
        two_sided(fwd, inv)
        for r in range(0, fs, CHUNK):
            for t in range(lane_tiles):
                cols = slice(t * LANES, (t + 1) * LANES)
                imag_cols = slice(fs + t * LANES, fs + (t + 1) * LANES)
                psi = []
                power = jnp.zeros((CHUNK, LANES), jnp.float32)
                for m in range(modes):
                    rows = slice(m * fs + r, m * fs + r + CHUNK)
                    real, imag = wide[rows, cols], wide[rows, imag_cols]
                    psi.append((real, imag))
                    power = power + (real * real + imag * imag)
                amp = amp_ref[slot, r : r + CHUNK, cols].astype(jnp.float32)
                factor = 1.0 - amp * lax.rsqrt(jnp.maximum(power, 0.25))
                for m in range(modes):
                    out = slice(m * fs + t * LANES, m * fs + (t + 1) * LANES)
                    stage[r : r + CHUNK, out] = (psi[m][0] * factor).astype(jnp.bfloat16)
                    stage[fs + r : fs + r + CHUNK, out] = (psi[m][1] * factor).astype(jnp.bfloat16)
        two_sided(inv, fwd)
        for r in range(0, fs, CHUNK):
            grads = [[], []]
            for t in range(lane_tiles):
                cols = slice(t * LANES, (t + 1) * LANES)
                imag_cols = slice(fs + t * LANES, fs + (t + 1) * LANES)
                patch_real = patch[0, r : r + CHUNK, cols]
                patch_imag = patch[1, r : r + CHUNK, cols]
                total_real = total_imag = 0.0
                for m in range(modes):
                    rows = slice(m * fs + r, m * fs + r + CHUNK)
                    real, imag = wide[rows, cols], wide[rows, imag_cols]
                    probe_real = probe_ref[0, m, r : r + CHUNK, cols]
                    probe_imag = probe_ref[1, m, r : r + CHUNK, cols]
                    total_real = total_real + (probe_real * real + probe_imag * imag)
                    total_imag = total_imag + (probe_real * imag - probe_imag * real)
                    at = (m * lane_tiles + t) * fs + r
                    pacc_ref[at : at + CHUNK, :] += patch_real * real + patch_imag * imag
                    at += modes * lane_tiles * fs
                    pacc_ref[at : at + CHUNK, :] += patch_real * imag - patch_imag * real
                grads[0].append(pltpu.roll(total_real, shift, 1))
                grads[1].append(pltpu.roll(total_imag, shift, 1))
            for plane in range(2):
                rolled = grads[plane]
                for t in range(lane_tiles + 1):
                    same = rolled[t] if t < lane_tiles else 0.0
                    before = rolled[t - 1] if t > 0 else 0.0
                    where = (plane, tile_at + t, pl.ds(row_at + r, CHUNK), slice(None))
                    acc_ref[where] += jnp.where(from_same, same, before)
        return carry

    lax.fori_loop(0, count_ref[0], advance, 0)


def frames_call(extended, probe_modes, amplitudes, positions, live_count, tables):
    fs = probe_modes.shape[-1]
    modes = probe_modes.shape[1]
    tiled = (2, extended.shape[1] + 1, extended.shape[2], LANES)
    vmem = pl.BlockSpec(memory_space=pltpu.VMEM)
    smem = pl.BlockSpec(memory_space=pltpu.SMEM)
    return pl.pallas_call(
        frames_kernel,
        out_shape=(
            jax.ShapeDtypeStruct(tiled, jnp.float32),
            jax.ShapeDtypeStruct((probe_modes.size // LANES, LANES), jnp.float32),
        ),
        in_specs=[smem, smem, vmem, vmem, vmem, vmem, vmem],
        out_specs=(vmem, vmem),
        scratch_shapes=[
            pltpu.VMEM(tiled, jnp.float32),
            pltpu.VMEM((2 * fs, 2 * fs), jnp.bfloat16),
            pltpu.VMEM((2 * fs, 2 * fs), jnp.bfloat16),
            pltpu.VMEM((2 * fs, modes * fs), jnp.bfloat16),
            pltpu.VMEM((modes * fs, 2 * fs), jnp.bfloat16),
            pltpu.VMEM((modes * fs, 2 * fs), jnp.float32),
            pltpu.VMEM((2, fs, fs), jnp.float32),
        ],
        compiler_params=pltpu.CompilerParams(vmem_limit_bytes=56 * 1024 * 1024),
        name="frames",
    )(live_count.reshape(1), positions, extended, probe_modes, amplitudes, *tables)


def shards(object_field, probe_modes, measured_amp, scan_positions, frame_counts):
    slot_count = measured_amp.shape[2]
    extended = halo_call(object_field)
    acc, probe_flat = frames_call(
        extended,
        probe_modes,
        measured_amp[0, 0],
        scan_positions[0, 0],
        frame_counts[0, 0],
        fourier_tables(probe_modes.shape[-1]),
    )
    norm_scale = 1.0 / math.sqrt(lax.axis_size("row") * lax.axis_size("col") * slot_count)
    return reduce_call(acc, probe_flat, object_field.shape, probe_modes.shape, norm_scale)


def solution(mesh):
    in_specs = (
        P(None, "row", "col"),
        P(),
        P("row", "col", None, None, None),
        P("row", "col", None, None),
        P("row", "col"),
    )
    out_specs = (P(None, "row", "col"), P())
    return jax.shard_map(shards, mesh=mesh, in_specs=in_specs, out_specs=out_specs, check_vma=False)
```

```python
import functools
import math

import jax
import jax.numpy as jnp
import numpy as np
from jax import lax
from jax.experimental import pallas as pl
from jax.experimental.pallas import tpu as pltpu
from jax.sharding import PartitionSpec as P

HALO = 128
LANES = 128


MESH = pl.DeviceIdType.MESH
SIDES = [(dr, dc) for dr in (-1, 0, 1) for dc in (-1, 0, 1) if (dr, dc) != (0, 0)]


def position():
    return (
        lax.axis_index("row"),
        lax.axis_index("col"),
        lax.axis_size("row"),
        lax.axis_size("col"),
    )


def exists(side):
    row, col, rows, cols = position()
    dr, dc = side
    inside = jnp.bool_(True)
    if dr:
        inside = row + dr >= 0 if dr < 0 else row + dr < rows
    if dc:
        other = col + dc >= 0 if dc < 0 else col + dc < cols
        inside = jnp.logical_and(inside, other) if dr else other
    return inside


def at_side(side):
    row, col, _, _ = position()
    return (row + side[0], col + side[1])


def opposite(side):
    return (-side[0], -side[1])


def part(step, margin, inner):
    return {-1: slice(0, margin), 0: slice(margin, margin + inner), 1: slice(margin + inner, None)}[
        step
    ]


def edge(step, margin, inner):
    return {-1: slice(0, margin), 0: slice(0, inner), 1: slice(inner - margin, inner)}[step]


def to_side(side, index, source, landing, send_sems, recv_sems):
    return pltpu.make_async_remote_copy(
        src_ref=source,
        dst_ref=landing,
        send_sem=send_sems.at[index],
        recv_sem=recv_sems.at[index],
        device_id=at_side(side),
        device_id_type=MESH,
    )


def halo_kernel(object_ref, ext_ref, *scratch):
    landings, (send_sems, recv_sems) = scratch[: len(SIDES)], scratch[len(SIDES) :]
    side_rows, side_cols = object_ref.shape[1:]
    barrier = pltpu.get_barrier_semaphore()
    count = jnp.int32(0)
    for side in SIDES:

        @pl.when(exists(side))
        def _(side=side):
            pl.semaphore_signal(barrier, inc=1, device_id=at_side(side), device_id_type=MESH)

        count = count + exists(side).astype(jnp.int32)
    pl.semaphore_wait(barrier, count)

    def copy(index):
        dr, dc = SIDES[index]
        source = object_ref.at[:, edge(dr, HALO, side_rows), edge(dc, HALO, side_cols)]
        return to_side(SIDES[index], index, source, landings[index], send_sems, recv_sems)

    for index, side in enumerate(SIDES):

        @pl.when(exists(side))
        def _(index=index):
            copy(index).start()

    for t in range(side_cols // LANES):
        ext_ref[:, HALO // LANES + t, HALO : HALO + side_rows, :] = object_ref[
            :, :, t * LANES : (t + 1) * LANES
        ]
    for index, side in enumerate(SIDES):
        dr, dc = opposite(side)
        rows = part(dr, HALO, side_rows)
        tiles = range(ext_ref.shape[1])[part(dc, HALO // LANES, side_cols // LANES)]

        @pl.when(exists((dr, dc)))
        def _(index=index, rows=rows, tiles=tiles):
            copy(index).wait_recv()
            for k, t in enumerate(tiles):
                ext_ref[:, t, rows, :] = landings[index][:, :, k * LANES : (k + 1) * LANES]

        @pl.when(jnp.logical_not(exists((dr, dc))))
        def _(rows=rows, tiles=tiles, index=index):
            for t in tiles:
                ext_ref[:, t, rows, :] = jnp.zeros(
                    (2, landings[index].shape[1], LANES), ext_ref.dtype
                )

    for index, side in enumerate(SIDES):

        @pl.when(exists(side))
        def _(index=index):
            copy(index).wait_send()


def halo_call(object_field):
    _, side_rows, side_cols = object_field.shape
    vmem = pl.BlockSpec(memory_space=pltpu.VMEM)
    landings = []
    for dr, dc in SIDES:
        landings.append(
            pltpu.VMEM((2, HALO if dr else side_rows, HALO if dc else side_cols), object_field.dtype)
        )
    sems = pltpu.SemaphoreType.DMA((len(SIDES),))
    return pl.pallas_call(
        halo_kernel,
        out_shape=jax.ShapeDtypeStruct(
            (2, (side_cols + 2 * HALO) // LANES, side_rows + 2 * HALO, LANES), object_field.dtype
        ),
        in_specs=[vmem],
        out_specs=vmem,
        scratch_shapes=landings + [sems, sems],
        compiler_params=pltpu.CompilerParams(
            collective_id=0, has_side_effects=True, vmem_limit_bytes=10 * 1024 * 1024
        ),
        name="halo",
    )(object_field)


def reduce_kernel(scale, acc_ref, pacc_ref, grad_ref, probe_ref, *scratch):
    count = len(SIDES)
    sends, landings, rest = scratch[:count], scratch[count : 2 * count], scratch[2 * count :]
    psend, precv, zsend, zrecv, full, side_sems, col_sems, row_sems = rest
    row, col, n_row, n_col = position()
    side_rows, side_cols = grad_ref.shape[1:]
    margin = HALO // LANES
    inner = side_cols // LANES
    for index, (dr, dc) in enumerate(SIDES):
        tiles = range(inner + 2 * margin)[part(dc, margin, inner)]
        rows = part(dr, HALO, side_rows)
        for k, t in enumerate(tiles):
            sends[index][:, k] = acc_ref[:, t, rows, :].astype(jnp.bfloat16)
    psend[...] = pacc_ref[...].astype(jnp.bfloat16)

    barrier = pltpu.get_barrier_semaphore()
    waits = jnp.int32(n_row + n_col - 2)
    for k in range(1, n_col):
        pl.semaphore_signal(
            barrier, inc=1, device_id=(row, lax.rem(col + k, n_col)), device_id_type=MESH
        )
    for k in range(1, n_row):
        pl.semaphore_signal(
            barrier, inc=1, device_id=(lax.rem(row + k, n_row), col), device_id_type=MESH
        )
    for side in SIDES:
        if side[0] and side[1]:

            @pl.when(exists(side))
            def _(side=side):
                pl.semaphore_signal(barrier, inc=1, device_id=at_side(side), device_id_type=MESH)

            waits = waits + exists(side).astype(jnp.int32)
    pl.semaphore_wait(barrier, waits)

    share = psend.shape[0] // n_col
    piece = share // n_row

    def to_peer(source, landing, sems, which, k, device):
        return pltpu.make_async_remote_copy(
            src_ref=source,
            dst_ref=landing,
            send_sem=sems.at[which, k - 1],
            recv_sem=sems.at[which + 1, k - 1],
            device_id=device,
            device_id_type=MESH,
        )

    def col_peer(k):
        return (row, lax.rem(col + k, n_col))

    def row_peer(k):
        return (lax.rem(row + k, n_row), col)

    def share_of(ref, index):
        return ref.at[pl.ds(pl.multiple_of(index * share, share), share)]

    def scatter_copy(k):
        return to_peer(
            share_of(psend, lax.rem(col + k, n_col)), precv.at[k - 1], col_sems, 0, k, col_peer(k)
        )

    def row_scatter_copy(k):
        target = lax.rem(row + k, n_row)
        return to_peer(
            zsend.at[pl.ds(pl.multiple_of(target * piece, piece), piece)],
            zrecv.at[k - 1],
            row_sems,
            0,
            k,
            row_peer(k),
        )

    def piece_of(index):
        start = pl.multiple_of(col * share + index * piece, piece)
        return full.at[pl.ds(start, piece)]

    def row_gather_copy(k, owner):
        return to_peer(piece_of(row), piece_of(owner), row_sems, 2, k, row_peer(k))

    def gather_copy(k, owner):
        return to_peer(share_of(full, col), share_of(full, owner), col_sems, 2, k, col_peer(k))

    def side_copy(index):
        return to_side(
            SIDES[index], index, sends[index], landings[index], side_sems.at[0], side_sems.at[1]
        )

    for k in range(1, n_col):
        scatter_copy(k).start()

    def start_sides(chosen):
        for index, side in enumerate(SIDES):
            if chosen(side):

                @pl.when(exists(side))
                def _(index=index):
                    side_copy(index).start()

    start_sides(lambda side: side[1] == 0)
    for t in range(inner):
        grad_ref[:, :, t * LANES : (t + 1) * LANES] = acc_ref[
            :, margin + t, HALO : HALO + side_rows, :
        ]
    total = pacc_ref[pl.ds(pl.multiple_of(col * share, share), share), :]
    for k in range(1, n_col):
        scatter_copy(k).wait_recv()
        total = total + precv[k - 1].astype(jnp.float32)
    zsend[...] = total
    for k in range(1, n_row):
        row_scatter_copy(k).start()
    start_sides(lambda side: side[0] == 0)
    start_sides(lambda side: side[0] != 0 and side[1] != 0)
    own = zsend[pl.ds(pl.multiple_of(row * piece, piece), piece), :]
    for k in range(1, n_row):
        row_scatter_copy(k).wait_recv()
        own = own + zrecv[k - 1]
    start = pl.multiple_of(col * share + row * piece, piece)
    full[pl.ds(start, piece), :] = (own * scale).astype(jnp.bfloat16)
    for k in range(1, n_row):
        row_gather_copy(k, row).start()
    for k in range(1, n_row):
        row_gather_copy(k, lax.rem(row + n_row - k, n_row)).wait_recv()
    for k in range(1, n_col):
        gather_copy(k, col).start()

    for index, side in enumerate(SIDES):
        dr, dc = opposite(side)
        rows = edge(dr, HALO, side_rows)
        tiles = range(inner)[edge(dc, margin, inner)]

        @pl.when(exists((dr, dc)))
        def _(index=index, rows=rows, tiles=tiles):
            side_copy(index).wait_recv()
            for k, t in enumerate(tiles):
                grad_ref[:, rows, t * LANES : (t + 1) * LANES] += landings[index][:, k].astype(
                    jnp.float32
                )

    for k in range(1, n_col):
        gather_copy(k, lax.rem(col + n_col - k, n_col)).wait_recv()
    parts, modes, fs, width = probe_ref.shape
    at = 0
    for p in range(parts):
        for m in range(modes):
            for t in range(width // LANES):
                probe_ref[p, m, :, t * LANES : (t + 1) * LANES] = full[at : at + fs, :].astype(
                    jnp.float32
                )
                at += fs
    for k in range(1, n_col):
        scatter_copy(k).wait_send()
        gather_copy(k, col).wait_send()
    for k in range(1, n_row):
        row_scatter_copy(k).wait_send()
        row_gather_copy(k, row).wait_send()
    for index, side in enumerate(SIDES):

        @pl.when(exists(side))
        def _(index=index):
            side_copy(index).wait_send()


def reduce_call(acc, probe_flat, object_shape, probe_shape, scale):
    n_row, n_col = lax.axis_size("row"), lax.axis_size("col")
    _, side_rows, side_cols = object_shape
    inner = side_cols // LANES
    margin = HALO // LANES
    vmem = pl.BlockSpec(memory_space=pltpu.VMEM)
    buffers = []
    for dr, dc in SIDES:
        buffers.append(
            pltpu.VMEM(
                (2, margin if dc else inner, HALO if dr else side_rows, LANES), jnp.bfloat16
            )
        )
    total_rows = probe_flat.shape[0]
    share = total_rows // n_col
    piece = share // n_row
    return pl.pallas_call(
        functools.partial(reduce_kernel, scale),
        out_shape=(
            jax.ShapeDtypeStruct(object_shape, jnp.float32),
            jax.ShapeDtypeStruct(probe_shape, jnp.float32),
        ),
        in_specs=[vmem, vmem],
        out_specs=(vmem, vmem),
        scratch_shapes=buffers
        + buffers
        + [
            pltpu.VMEM((total_rows, LANES), jnp.bfloat16),
            pltpu.VMEM((n_col - 1, share, LANES), jnp.bfloat16),
            pltpu.VMEM((share, LANES), jnp.float32),
            pltpu.VMEM((n_row - 1, piece, LANES), jnp.float32),
            pltpu.VMEM((total_rows, LANES), jnp.bfloat16),
            pltpu.SemaphoreType.DMA((2, len(SIDES))),
            pltpu.SemaphoreType.DMA((4, n_col - 1)),
            pltpu.SemaphoreType.DMA((4, n_row - 1)),
        ],
        compiler_params=pltpu.CompilerParams(
            collective_id=1, has_side_effects=True, vmem_limit_bytes=20 * 1024 * 1024
        ),
        name="reduce",
    )(acc, probe_flat)


def fourier_tables(frame_side):
    indices = np.arange(frame_side)
    product = indices[:, None] * indices[None, :] % frame_side
    angles = 2.0 * math.pi / frame_side * product
    norm_scale = 1.0 / math.sqrt(frame_side)
    return (
        jnp.asarray((np.cos(angles) * norm_scale).astype(np.float32)).astype(jnp.bfloat16),
        jnp.asarray((-np.sin(angles) * norm_scale).astype(np.float32)).astype(jnp.bfloat16),
    )


CHUNK = 32


def dot32(left, right):
    return jnp.dot(left, right, preferred_element_type=jnp.float32)


def frames_kernel(
    count_ref, at_ref, ext_ref, probe_ref, amp_ref, tr_ref, ti_ref, acc_ref, pacc_ref,
    extf, fwd, inv, stage, half, wide, patch,
):
    fs = probe_ref.shape[-1]
    modes = probe_ref.shape[1]
    tiles = ext_ref.shape[1]
    lane_tiles = fs // LANES
    for plane in range(2):
        for t in range(tiles):
            extf[plane, t] = ext_ref[plane, t].astype(jnp.float32)
        extf[plane, tiles] = jnp.zeros(extf.shape[2:], jnp.float32)
    acc_ref[...] = jnp.zeros(acc_ref.shape, jnp.float32)
    pacc_ref[...] = jnp.zeros(pacc_ref.shape, jnp.float32)
    table_real, table_imag = tr_ref[...], ti_ref[...]
    minus = -table_imag
    fwd[:fs, :fs] = table_real
    fwd[:fs, fs:] = minus
    fwd[fs:, :fs] = table_imag
    fwd[fs:, fs:] = table_real
    inv[:fs, :fs] = table_real
    inv[:fs, fs:] = table_imag
    inv[fs:, :fs] = minus
    inv[fs:, fs:] = table_real

    def two_sided(left_table, right_table):
        for m in range(modes):
            both = dot32(left_table[...], stage[:, m * fs : (m + 1) * fs])
            half[m * fs : (m + 1) * fs, :fs] = both[:fs].astype(jnp.bfloat16)
            half[m * fs : (m + 1) * fs, fs:] = both[fs:].astype(jnp.bfloat16)
        wide[...] = dot32(half[...], right_table[...])

    def advance(slot, carry):
        row_at = at_ref[0, slot]
        col_at = at_ref[1, slot]
        tile_at = col_at // LANES
        shift = col_at % LANES
        back_shift = (LANES - shift) % LANES
        lane = lax.broadcasted_iota(jnp.int32, (CHUNK, LANES), 1)
        keep_low = lane < LANES - shift
        from_same = lane >= shift
        for r in range(0, fs, CHUNK):
            rows = slice(r, r + CHUNK)
            values = []
            for plane in range(2):
                rolled = [
                    pltpu.roll(
                        extf[plane, tile_at + t, pl.ds(row_at + r, CHUNK), :], back_shift, 1
                    )
                    for t in range(lane_tiles + 1)
                ]
                values.append(
                    [jnp.where(keep_low, rolled[t], rolled[t + 1]) for t in range(lane_tiles)]
                )
            for t in range(lane_tiles):
                cols = slice(t * LANES, (t + 1) * LANES)
                patch_real, patch_imag = values[0][t], values[1][t]
                patch[0, rows, cols] = patch_real
                patch[1, rows, cols] = patch_imag
                for m in range(modes):
                    probe_real = probe_ref[0, m, rows, cols]
                    probe_imag = probe_ref[1, m, rows, cols]
                    out = slice(m * fs + t * LANES, m * fs + (t + 1) * LANES)
                    stage[rows, out] = (
                        probe_real * patch_real - probe_imag * patch_imag
                    ).astype(jnp.bfloat16)
                    stage[fs + r : fs + r + CHUNK, out] = (
                        probe_real * patch_imag + probe_imag * patch_real
                    ).astype(jnp.bfloat16)
        two_sided(fwd, inv)
        for r in range(0, fs, CHUNK):
            for t in range(lane_tiles):
                cols = slice(t * LANES, (t + 1) * LANES)
                imag_cols = slice(fs + t * LANES, fs + (t + 1) * LANES)
                psi = []
                power = jnp.zeros((CHUNK, LANES), jnp.float32)
                for m in range(modes):
                    rows = slice(m * fs + r, m * fs + r + CHUNK)
                    real, imag = wide[rows, cols], wide[rows, imag_cols]
                    psi.append((real, imag))
                    power = power + (real * real + imag * imag)
                amp = amp_ref[slot, r : r + CHUNK, cols].astype(jnp.float32)
                factor = 1.0 - amp * lax.rsqrt(jnp.maximum(power, 0.25))
                for m in range(modes):
                    out = slice(m * fs + t * LANES, m * fs + (t + 1) * LANES)
                    stage[r : r + CHUNK, out] = (psi[m][0] * factor).astype(jnp.bfloat16)
                    stage[fs + r : fs + r + CHUNK, out] = (psi[m][1] * factor).astype(jnp.bfloat16)
        two_sided(inv, fwd)
        for r in range(0, fs, CHUNK):
            grads = [[], []]
            for t in range(lane_tiles):
                cols = slice(t * LANES, (t + 1) * LANES)
                imag_cols = slice(fs + t * LANES, fs + (t + 1) * LANES)
                patch_real = patch[0, r : r + CHUNK, cols]
                patch_imag = patch[1, r : r + CHUNK, cols]
                total_real = total_imag = 0.0
                for m in range(modes):
                    rows = slice(m * fs + r, m * fs + r + CHUNK)
                    real, imag = wide[rows, cols], wide[rows, imag_cols]
                    probe_real = probe_ref[0, m, r : r + CHUNK, cols]
                    probe_imag = probe_ref[1, m, r : r + CHUNK, cols]
                    total_real = total_real + (probe_real * real + probe_imag * imag)
                    total_imag = total_imag + (probe_real * imag - probe_imag * real)
                    at = (m * lane_tiles + t) * fs + r
                    pacc_ref[at : at + CHUNK, :] += patch_real * real + patch_imag * imag
                    at += modes * lane_tiles * fs
                    pacc_ref[at : at + CHUNK, :] += patch_real * imag - patch_imag * real
                grads[0].append(pltpu.roll(total_real, shift, 1))
                grads[1].append(pltpu.roll(total_imag, shift, 1))
            for plane in range(2):
                rolled = grads[plane]
                for t in range(lane_tiles + 1):
                    same = rolled[t] if t < lane_tiles else 0.0
                    before = rolled[t - 1] if t > 0 else 0.0
                    where = (plane, tile_at + t, pl.ds(row_at + r, CHUNK), slice(None))
                    acc_ref[where] += jnp.where(from_same, same, before)
        return carry

    lax.fori_loop(0, count_ref[0], advance, 0)


def frames_call(extended, probe_modes, amplitudes, positions, live_count, tables):
    fs = probe_modes.shape[-1]
    modes = probe_modes.shape[1]
    tiled = (2, extended.shape[1] + 1, extended.shape[2], LANES)
    vmem = pl.BlockSpec(memory_space=pltpu.VMEM)
    smem = pl.BlockSpec(memory_space=pltpu.SMEM)
    return pl.pallas_call(
        frames_kernel,
        out_shape=(
            jax.ShapeDtypeStruct(tiled, jnp.float32),
            jax.ShapeDtypeStruct((probe_modes.size // LANES, LANES), jnp.float32),
        ),
        in_specs=[smem, smem, vmem, vmem, vmem, vmem, vmem],
        out_specs=(vmem, vmem),
        scratch_shapes=[
            pltpu.VMEM(tiled, jnp.float32),
            pltpu.VMEM((2 * fs, 2 * fs), jnp.bfloat16),
            pltpu.VMEM((2 * fs, 2 * fs), jnp.bfloat16),
            pltpu.VMEM((2 * fs, modes * fs), jnp.bfloat16),
            pltpu.VMEM((modes * fs, 2 * fs), jnp.bfloat16),
            pltpu.VMEM((modes * fs, 2 * fs), jnp.float32),
            pltpu.VMEM((2, fs, fs), jnp.float32),
        ],
        compiler_params=pltpu.CompilerParams(vmem_limit_bytes=26 * 1024 * 1024),
        name="frames",
    )(live_count.reshape(1), positions, extended, probe_modes, amplitudes, *tables)


def shards(object_field, probe_modes, measured_amp, scan_positions, frame_counts):
    slot_count = measured_amp.shape[2]
    extended = halo_call(object_field)
    acc, probe_flat = frames_call(
        extended,
        probe_modes,
        measured_amp[0, 0],
        scan_positions[0, 0],
        frame_counts[0, 0],
        fourier_tables(probe_modes.shape[-1]),
    )
    norm_scale = 1.0 / math.sqrt(lax.axis_size("row") * lax.axis_size("col") * slot_count)
    return reduce_call(acc, probe_flat, object_field.shape, probe_modes.shape, norm_scale)


def solution(mesh):
    in_specs = (
        P(None, "row", "col"),
        P(),
        P("row", "col", None, None, None),
        P("row", "col", None, None),
        P("row", "col"),
    )
    out_specs = (P(None, "row", "col"), P())
    return jax.shard_map(shards, mesh=mesh, in_specs=in_specs, out_specs=out_specs, check_vma=False)
```

```python
import functools
import math

import jax
import jax.numpy as jnp
import numpy as np
from jax import lax
from jax.experimental import pallas as pl
from jax.experimental.pallas import tpu as pltpu
from jax.sharding import PartitionSpec as P

HALO = 128
LANES = 128


MESH = pl.DeviceIdType.MESH
SIDES = [(dr, dc) for dr in (-1, 0, 1) for dc in (-1, 0, 1) if (dr, dc) != (0, 0)]


def position():
    return (
        lax.axis_index("row"),
        lax.axis_index("col"),
        lax.axis_size("row"),
        lax.axis_size("col"),
    )


def exists(side):
    row, col, rows, cols = position()
    dr, dc = side
    inside = jnp.bool_(True)
    if dr:
        inside = row + dr >= 0 if dr < 0 else row + dr < rows
    if dc:
        other = col + dc >= 0 if dc < 0 else col + dc < cols
        inside = jnp.logical_and(inside, other) if dr else other
    return inside


def at_side(side):
    row, col, _, _ = position()
    return (row + side[0], col + side[1])


def opposite(side):
    return (-side[0], -side[1])


def part(step, margin, inner):
    return {-1: slice(0, margin), 0: slice(margin, margin + inner), 1: slice(margin + inner, None)}[
        step
    ]


def edge(step, margin, inner):
    return {-1: slice(0, margin), 0: slice(0, inner), 1: slice(inner - margin, inner)}[step]


def to_side(side, index, source, landing, send_sems, recv_sems):
    return pltpu.make_async_remote_copy(
        src_ref=source,
        dst_ref=landing,
        send_sem=send_sems.at[index],
        recv_sem=recv_sems.at[index],
        device_id=at_side(side),
        device_id_type=MESH,
    )


def halo_kernel(object_ref, ext_ref, *scratch):
    landings, (send_sems, recv_sems) = scratch[: len(SIDES)], scratch[len(SIDES) :]
    side_rows, side_cols = object_ref.shape[1:]
    barrier = pltpu.get_barrier_semaphore()
    count = jnp.int32(0)
    for side in SIDES:

        @pl.when(exists(side))
        def _(side=side):
            pl.semaphore_signal(barrier, inc=1, device_id=at_side(side), device_id_type=MESH)

        count = count + exists(side).astype(jnp.int32)
    pl.semaphore_wait(barrier, count)

    def copy(index):
        dr, dc = SIDES[index]
        source = object_ref.at[:, edge(dr, HALO, side_rows), edge(dc, HALO, side_cols)]
        return to_side(SIDES[index], index, source, landings[index], send_sems, recv_sems)

    for index, side in enumerate(SIDES):

        @pl.when(exists(side))
        def _(index=index):
            copy(index).start()

    for t in range(side_cols // LANES):
        ext_ref[:, HALO // LANES + t, HALO : HALO + side_rows, :] = object_ref[
            :, :, t * LANES : (t + 1) * LANES
        ].astype(jnp.float32)
    spare = ext_ref.shape[1] - 1
    ext_ref[:, spare] = jnp.zeros((2, ext_ref.shape[2], LANES), jnp.float32)
    for index, side in enumerate(SIDES):
        dr, dc = opposite(side)
        rows = part(dr, HALO, side_rows)
        tiles = range(spare)[part(dc, HALO // LANES, side_cols // LANES)]

        @pl.when(exists((dr, dc)))
        def _(index=index, rows=rows, tiles=tiles):
            copy(index).wait_recv()
            for k, t in enumerate(tiles):
                ext_ref[:, t, rows, :] = landings[index][
                    :, :, k * LANES : (k + 1) * LANES
                ].astype(jnp.float32)

        @pl.when(jnp.logical_not(exists((dr, dc))))
        def _(rows=rows, tiles=tiles, index=index):
            for t in tiles:
                ext_ref[:, t, rows, :] = jnp.zeros(
                    (2, landings[index].shape[1], LANES), ext_ref.dtype
                )

    for index, side in enumerate(SIDES):

        @pl.when(exists(side))
        def _(index=index):
            copy(index).wait_send()


def halo_call(object_field):
    _, side_rows, side_cols = object_field.shape
    vmem = pl.BlockSpec(memory_space=pltpu.VMEM)
    landings = []
    for dr, dc in SIDES:
        landings.append(
            pltpu.VMEM((2, HALO if dr else side_rows, HALO if dc else side_cols), object_field.dtype)
        )
    sems = pltpu.SemaphoreType.DMA((len(SIDES),))
    return pl.pallas_call(
        halo_kernel,
        out_shape=jax.ShapeDtypeStruct(
            (2, (side_cols + 2 * HALO) // LANES + 1, side_rows + 2 * HALO, LANES), jnp.float32
        ),
        in_specs=[vmem],
        out_specs=vmem,
        scratch_shapes=landings + [sems, sems],
        compiler_params=pltpu.CompilerParams(
            collective_id=0, has_side_effects=True, vmem_limit_bytes=14 * 1024 * 1024
        ),
        name="halo",
    )(object_field)


def reduce_kernel(scale, acc_ref, pacc_ref, grad_ref, probe_ref, *scratch):
    count = len(SIDES)
    sends, landings, rest = scratch[:count], scratch[count : 2 * count], scratch[2 * count :]
    psend, precv, zsend, zrecv, full, side_sems, col_sems, row_sems = rest
    row, col, n_row, n_col = position()
    side_rows, side_cols = grad_ref.shape[1:]
    margin = HALO // LANES
    inner = side_cols // LANES
    for index, (dr, dc) in enumerate(SIDES):
        tiles = range(inner + 2 * margin)[part(dc, margin, inner)]
        rows = part(dr, HALO, side_rows)
        for k, t in enumerate(tiles):
            sends[index][:, k] = acc_ref[:, t, rows, :].astype(jnp.bfloat16)
    psend[...] = pacc_ref[...].astype(jnp.bfloat16)

    barrier = pltpu.get_barrier_semaphore()
    waits = jnp.int32(n_row + n_col - 2)
    for k in range(1, n_col):
        pl.semaphore_signal(
            barrier, inc=1, device_id=(row, lax.rem(col + k, n_col)), device_id_type=MESH
        )
    for k in range(1, n_row):
        pl.semaphore_signal(
            barrier, inc=1, device_id=(lax.rem(row + k, n_row), col), device_id_type=MESH
        )
    for side in SIDES:
        if side[0] and side[1]:

            @pl.when(exists(side))
            def _(side=side):
                pl.semaphore_signal(barrier, inc=1, device_id=at_side(side), device_id_type=MESH)

            waits = waits + exists(side).astype(jnp.int32)
    pl.semaphore_wait(barrier, waits)

    share = psend.shape[0] // n_col
    piece = share // n_row

    def to_peer(source, landing, sems, which, k, device):
        return pltpu.make_async_remote_copy(
            src_ref=source,
            dst_ref=landing,
            send_sem=sems.at[which, k - 1],
            recv_sem=sems.at[which + 1, k - 1],
            device_id=device,
            device_id_type=MESH,
        )

    def col_peer(k):
        return (row, lax.rem(col + k, n_col))

    def row_peer(k):
        return (lax.rem(row + k, n_row), col)

    def share_of(ref, index):
        return ref.at[pl.ds(pl.multiple_of(index * share, share), share)]

    def scatter_copy(k):
        return to_peer(
            share_of(psend, lax.rem(col + k, n_col)), precv.at[k - 1], col_sems, 0, k, col_peer(k)
        )

    def row_scatter_copy(k):
        target = lax.rem(row + k, n_row)
        return to_peer(
            zsend.at[pl.ds(pl.multiple_of(target * piece, piece), piece)],
            zrecv.at[k - 1],
            row_sems,
            0,
            k,
            row_peer(k),
        )

    def piece_of(index):
        start = pl.multiple_of(col * share + index * piece, piece)
        return full.at[pl.ds(start, piece)]

    def row_gather_copy(k, owner):
        return to_peer(piece_of(row), piece_of(owner), row_sems, 2, k, row_peer(k))

    def gather_copy(k, owner):
        return to_peer(share_of(full, col), share_of(full, owner), col_sems, 2, k, col_peer(k))

    def side_copy(index):
        return to_side(
            SIDES[index], index, sends[index], landings[index], side_sems.at[0], side_sems.at[1]
        )

    for k in range(1, n_col):
        scatter_copy(k).start()

    def start_sides(chosen):
        for index, side in enumerate(SIDES):
            if chosen(side):

                @pl.when(exists(side))
                def _(index=index):
                    side_copy(index).start()

    start_sides(lambda side: side[1] == 0)
    for t in range(inner):
        grad_ref[:, :, t * LANES : (t + 1) * LANES] = acc_ref[
            :, margin + t, HALO : HALO + side_rows, :
        ]
    total = pacc_ref[pl.ds(pl.multiple_of(col * share, share), share), :]
    for k in range(1, n_col):
        scatter_copy(k).wait_recv()
        total = total + precv[k - 1].astype(jnp.float32)
    zsend[...] = total
    for k in range(1, n_row):
        row_scatter_copy(k).start()
    start_sides(lambda side: side[0] == 0)
    start_sides(lambda side: side[0] != 0 and side[1] != 0)
    own = zsend[pl.ds(pl.multiple_of(row * piece, piece), piece), :]
    for k in range(1, n_row):
        row_scatter_copy(k).wait_recv()
        own = own + zrecv[k - 1]
    start = pl.multiple_of(col * share + row * piece, piece)
    full[pl.ds(start, piece), :] = (own * scale).astype(jnp.bfloat16)
    for k in range(1, n_row):
        row_gather_copy(k, row).start()
    for k in range(1, n_row):
        row_gather_copy(k, lax.rem(row + n_row - k, n_row)).wait_recv()
    for k in range(1, n_col):
        gather_copy(k, col).start()

    for index, side in enumerate(SIDES):
        dr, dc = opposite(side)
        rows = edge(dr, HALO, side_rows)
        tiles = range(inner)[edge(dc, margin, inner)]

        @pl.when(exists((dr, dc)))
        def _(index=index, rows=rows, tiles=tiles):
            side_copy(index).wait_recv()
            for k, t in enumerate(tiles):
                grad_ref[:, rows, t * LANES : (t + 1) * LANES] += landings[index][:, k].astype(
                    jnp.float32
                )

    for k in range(1, n_col):
        gather_copy(k, lax.rem(col + n_col - k, n_col)).wait_recv()
    parts, modes, fs, width = probe_ref.shape
    at = 0
    for p in range(parts):
        for m in range(modes):
            for t in range(width // LANES):
                probe_ref[p, m, :, t * LANES : (t + 1) * LANES] = full[at : at + fs, :].astype(
                    jnp.float32
                )
                at += fs
    for k in range(1, n_col):
        scatter_copy(k).wait_send()
        gather_copy(k, col).wait_send()
    for k in range(1, n_row):
        row_scatter_copy(k).wait_send()
        row_gather_copy(k, row).wait_send()
    for index, side in enumerate(SIDES):

        @pl.when(exists(side))
        def _(index=index):
            side_copy(index).wait_send()


def reduce_call(acc, probe_flat, object_shape, probe_shape, scale):
    n_row, n_col = lax.axis_size("row"), lax.axis_size("col")
    _, side_rows, side_cols = object_shape
    inner = side_cols // LANES
    margin = HALO // LANES
    vmem = pl.BlockSpec(memory_space=pltpu.VMEM)
    buffers = []
    for dr, dc in SIDES:
        buffers.append(
            pltpu.VMEM(
                (2, margin if dc else inner, HALO if dr else side_rows, LANES), jnp.bfloat16
            )
        )
    total_rows = probe_flat.shape[0]
    share = total_rows // n_col
    piece = share // n_row
    return pl.pallas_call(
        functools.partial(reduce_kernel, scale),
        out_shape=(
            jax.ShapeDtypeStruct(object_shape, jnp.float32),
            jax.ShapeDtypeStruct(probe_shape, jnp.float32),
        ),
        in_specs=[vmem, vmem],
        out_specs=(vmem, vmem),
        scratch_shapes=buffers
        + buffers
        + [
            pltpu.VMEM((total_rows, LANES), jnp.bfloat16),
            pltpu.VMEM((n_col - 1, share, LANES), jnp.bfloat16),
            pltpu.VMEM((share, LANES), jnp.float32),
            pltpu.VMEM((n_row - 1, piece, LANES), jnp.float32),
            pltpu.VMEM((total_rows, LANES), jnp.bfloat16),
            pltpu.SemaphoreType.DMA((2, len(SIDES))),
            pltpu.SemaphoreType.DMA((4, n_col - 1)),
            pltpu.SemaphoreType.DMA((4, n_row - 1)),
        ],
        compiler_params=pltpu.CompilerParams(
            collective_id=1, has_side_effects=True, vmem_limit_bytes=20 * 1024 * 1024
        ),
        name="reduce",
    )(acc, probe_flat)


def fourier_tables(frame_side):
    indices = np.arange(frame_side)
    product = indices[:, None] * indices[None, :] % frame_side
    angles = 2.0 * math.pi / frame_side * product
    norm_scale = 1.0 / math.sqrt(frame_side)
    return (
        jnp.asarray((np.cos(angles) * norm_scale).astype(np.float32)).astype(jnp.bfloat16),
        jnp.asarray((-np.sin(angles) * norm_scale).astype(np.float32)).astype(jnp.bfloat16),
    )


CHUNK = 32


def dot32(left, right):
    return jnp.dot(left, right, preferred_element_type=jnp.float32)


def frames_kernel(
    count_ref, at_ref, ext_ref, probe_ref, amp_ref, tr_ref, ti_ref, acc_ref, pacc_ref,
    fwd, inv, *buffers,
):
    fs = probe_ref.shape[-1]
    modes = probe_ref.shape[1]
    lane_tiles = fs // LANES
    last_slot = amp_ref.shape[0] - 1
    live = count_ref[0]
    even, odd = buffers[:4], buffers[4:]
    acc_ref[...] = jnp.zeros(acc_ref.shape, jnp.float32)
    pacc_ref[...] = jnp.zeros(pacc_ref.shape, jnp.float32)
    odd[2][...] = jnp.zeros(odd[2].shape, jnp.float32)
    odd[3][...] = jnp.zeros(odd[3].shape, jnp.float32)
    table_real, table_imag = tr_ref[...], ti_ref[...]
    minus = -table_imag
    fwd[:fs, :fs] = table_real
    fwd[:fs, fs:] = minus
    fwd[fs:, :fs] = table_imag
    fwd[fs:, fs:] = table_real
    inv[:fs, :fs] = table_real
    inv[:fs, fs:] = table_imag
    inv[fs:, :fs] = minus
    inv[fs:, fs:] = table_real

    def two_sided(buffer, left_table, right_table):
        stage, half, wide, _ = buffer
        for m in range(modes):
            both = dot32(left_table[...], stage[:, m * fs : (m + 1) * fs])
            half[m * fs : (m + 1) * fs, :fs] = both[:fs].astype(jnp.bfloat16)
            half[m * fs : (m + 1) * fs, fs:] = both[fs:].astype(jnp.bfloat16)
        wide[...] = dot32(half[...], right_table[...])

    def make_exit(buffer, slot):
        stage, _, _, patch = buffer
        row_at = at_ref[0, slot]
        col_at = at_ref[1, slot]
        tile_at = col_at // LANES
        shift = col_at % LANES
        back_shift = (LANES - shift) % LANES
        lane = lax.broadcasted_iota(jnp.int32, (CHUNK, LANES), 1)
        keep_low = lane < LANES - shift
        for r in range(0, fs, CHUNK):
            rows = slice(r, r + CHUNK)
            values = []
            for plane in range(2):
                rolled = [
                    pltpu.roll(
                        ext_ref[plane, tile_at + t, pl.ds(row_at + r, CHUNK), :], back_shift, 1
                    )
                    for t in range(lane_tiles + 1)
                ]
                values.append(
                    [jnp.where(keep_low, rolled[t], rolled[t + 1]) for t in range(lane_tiles)]
                )
            for t in range(lane_tiles):
                cols = slice(t * LANES, (t + 1) * LANES)
                patch_real, patch_imag = values[0][t], values[1][t]
                patch[0, rows, cols] = patch_real
                patch[1, rows, cols] = patch_imag
                for m in range(modes):
                    probe_real = probe_ref[0, m, rows, cols]
                    probe_imag = probe_ref[1, m, rows, cols]
                    out = slice(m * fs + t * LANES, m * fs + (t + 1) * LANES)
                    stage[rows, out] = (
                        probe_real * patch_real - probe_imag * patch_imag
                    ).astype(jnp.bfloat16)
                    stage[fs + r : fs + r + CHUNK, out] = (
                        probe_real * patch_imag + probe_imag * patch_real
                    ).astype(jnp.bfloat16)

    def make_chi(buffer, slot, valid):
        stage, _, wide, _ = buffer
        for r in range(0, fs, CHUNK):
            for t in range(lane_tiles):
                cols = slice(t * LANES, (t + 1) * LANES)
                imag_cols = slice(fs + t * LANES, fs + (t + 1) * LANES)
                psi = []
                power = None
                for m in range(modes):
                    rows = slice(m * fs + r, m * fs + r + CHUNK)
                    real, imag = wide[rows, cols], wide[rows, imag_cols]
                    psi.append((real, imag))
                    own = real * real + imag * imag
                    power = own if power is None else power + own
                amp = amp_ref[slot, r : r + CHUNK, cols].astype(jnp.float32)
                factor = 1.0 - amp * lax.rsqrt(jnp.maximum(power, 0.25))
                if valid is not None:
                    factor = jnp.where(valid, factor, 0.0)
                for m in range(modes):
                    out = slice(m * fs + t * LANES, m * fs + (t + 1) * LANES)
                    stage[r : r + CHUNK, out] = (psi[m][0] * factor).astype(jnp.bfloat16)
                    stage[fs + r : fs + r + CHUNK, out] = (psi[m][1] * factor).astype(jnp.bfloat16)

    def add_grads(buffer, slot):
        _, _, wide, patch = buffer
        row_at = at_ref[0, slot]
        col_at = at_ref[1, slot]
        tile_at = col_at // LANES
        shift = col_at % LANES
        lane = lax.broadcasted_iota(jnp.int32, (CHUNK, LANES), 1)
        from_same = lane >= shift
        for r in range(0, fs, CHUNK):
            grads = [[], []]
            for t in range(lane_tiles):
                cols = slice(t * LANES, (t + 1) * LANES)
                imag_cols = slice(fs + t * LANES, fs + (t + 1) * LANES)
                patch_real = patch[0, r : r + CHUNK, cols]
                patch_imag = patch[1, r : r + CHUNK, cols]
                total_real = total_imag = None
                for m in range(modes):
                    rows = slice(m * fs + r, m * fs + r + CHUNK)
                    real, imag = wide[rows, cols], wide[rows, imag_cols]
                    probe_real = probe_ref[0, m, r : r + CHUNK, cols]
                    probe_imag = probe_ref[1, m, r : r + CHUNK, cols]
                    own_real = probe_real * real + probe_imag * imag
                    own_imag = probe_real * imag - probe_imag * real
                    total_real = own_real if m == 0 else total_real + own_real
                    total_imag = own_imag if m == 0 else total_imag + own_imag
                    at = (m * lane_tiles + t) * fs + r
                    pacc_ref[at : at + CHUNK, :] += patch_real * real + patch_imag * imag
                    at += modes * lane_tiles * fs
                    pacc_ref[at : at + CHUNK, :] += patch_real * imag - patch_imag * real
                grads[0].append(pltpu.roll(total_real, shift, 1))
                grads[1].append(pltpu.roll(total_imag, shift, 1))
            for plane in range(2):
                rolled = grads[plane]
                for t in range(lane_tiles + 1):
                    same = rolled[t] if t < lane_tiles else 0.0
                    before = rolled[t - 1] if t > 0 else 0.0
                    where = (plane, tile_at + t, pl.ds(row_at + r, CHUNK), slice(None))
                    acc_ref[where] += jnp.where(from_same, same, before)

    def advance(pair, carry):
        first = 2 * pair
        second = jnp.minimum(first + 1, last_slot)
        make_exit(even, first)
        two_sided(even, fwd, inv)
        add_grads(odd, jnp.maximum(first - 1, 0))
        make_exit(odd, second)
        two_sided(odd, fwd, inv)
        make_chi(even, first, None)
        two_sided(even, inv, fwd)
        make_chi(odd, second, first + 1 < live)
        two_sided(odd, inv, fwd)
        add_grads(even, first)
        return carry

    pairs = (live + 1) // 2
    lax.fori_loop(0, pairs, advance, 0)
    add_grads(odd, jnp.minimum(2 * pairs - 1, last_slot))


def frames_call(extended, probe_modes, amplitudes, positions, live_count, tables):
    fs = probe_modes.shape[-1]
    modes = probe_modes.shape[1]
    tiled = extended.shape
    vmem = pl.BlockSpec(memory_space=pltpu.VMEM)
    smem = pl.BlockSpec(memory_space=pltpu.SMEM)
    return pl.pallas_call(
        frames_kernel,
        out_shape=(
            jax.ShapeDtypeStruct(tiled, jnp.float32),
            jax.ShapeDtypeStruct((probe_modes.size // LANES, LANES), jnp.float32),
        ),
        in_specs=[smem, smem, vmem, vmem, vmem, vmem, vmem],
        out_specs=(vmem, vmem),
        scratch_shapes=[
            pltpu.VMEM((2 * fs, 2 * fs), jnp.bfloat16),
            pltpu.VMEM((2 * fs, 2 * fs), jnp.bfloat16),
        ]
        + 2
        * [
            pltpu.VMEM((2 * fs, modes * fs), jnp.bfloat16),
            pltpu.VMEM((modes * fs, 2 * fs), jnp.bfloat16),
            pltpu.VMEM((modes * fs, 2 * fs), jnp.float32),
            pltpu.VMEM((2, fs, fs), jnp.float32),
        ],
        compiler_params=pltpu.CompilerParams(vmem_limit_bytes=26 * 1024 * 1024),
        name="frames",
    )(live_count.reshape(1), positions, extended, probe_modes, amplitudes, *tables)


def shards(object_field, probe_modes, measured_amp, scan_positions, frame_counts):
    slot_count = measured_amp.shape[2]
    extended = halo_call(object_field)
    acc, probe_flat = frames_call(
        extended,
        probe_modes,
        measured_amp[0, 0],
        scan_positions[0, 0],
        frame_counts[0, 0],
        fourier_tables(probe_modes.shape[-1]),
    )
    norm_scale = 1.0 / math.sqrt(lax.axis_size("row") * lax.axis_size("col") * slot_count)
    return reduce_call(acc, probe_flat, object_field.shape, probe_modes.shape, norm_scale)


def solution(mesh):
    in_specs = (
        P(None, "row", "col"),
        P(),
        P("row", "col", None, None, None),
        P("row", "col", None, None),
        P("row", "col"),
    )
    out_specs = (P(None, "row", "col"), P())
    return jax.shard_map(shards, mesh=mesh, in_specs=in_specs, out_specs=out_specs, check_vma=False)
```

```python
import functools
import math

import jax
import jax.numpy as jnp
import numpy as np
from jax import lax
from jax.experimental import pallas as pl
from jax.experimental.pallas import tpu as pltpu
from jax.sharding import PartitionSpec as P

HALO = 128
LANES = 128


MESH = pl.DeviceIdType.MESH
SIDES = [(dr, dc) for dr in (-1, 0, 1) for dc in (-1, 0, 1) if (dr, dc) != (0, 0)]


def position():
    return (
        lax.axis_index("row"),
        lax.axis_index("col"),
        lax.axis_size("row"),
        lax.axis_size("col"),
    )


def exists(side):
    row, col, rows, cols = position()
    dr, dc = side
    inside = jnp.bool_(True)
    if dr:
        inside = row + dr >= 0 if dr < 0 else row + dr < rows
    if dc:
        other = col + dc >= 0 if dc < 0 else col + dc < cols
        inside = jnp.logical_and(inside, other) if dr else other
    return inside


def at_side(side):
    row, col, _, _ = position()
    return (row + side[0], col + side[1])


def opposite(side):
    return (-side[0], -side[1])


def part(step, margin, inner):
    return {-1: slice(0, margin), 0: slice(margin, margin + inner), 1: slice(margin + inner, None)}[
        step
    ]


def edge(step, margin, inner):
    return {-1: slice(0, margin), 0: slice(0, inner), 1: slice(inner - margin, inner)}[step]


def to_side(side, index, source, landing, send_sems, recv_sems):
    return pltpu.make_async_remote_copy(
        src_ref=source,
        dst_ref=landing,
        send_sem=send_sems.at[index],
        recv_sem=recv_sems.at[index],
        device_id=at_side(side),
        device_id_type=MESH,
    )


def halo_kernel(object_ref, ext_ref, *scratch):
    landings, (send_sems, recv_sems) = scratch[: len(SIDES)], scratch[len(SIDES) :]
    side_rows, side_cols = object_ref.shape[1:]
    barrier = pltpu.get_barrier_semaphore()
    count = jnp.int32(0)
    for side in SIDES:

        @pl.when(exists(side))
        def _(side=side):
            pl.semaphore_signal(barrier, inc=1, device_id=at_side(side), device_id_type=MESH)

        count = count + exists(side).astype(jnp.int32)
    pl.semaphore_wait(barrier, count)

    def copy(index):
        dr, dc = SIDES[index]
        source = object_ref.at[:, edge(dr, HALO, side_rows), edge(dc, HALO, side_cols)]
        return to_side(SIDES[index], index, source, landings[index], send_sems, recv_sems)

    for index, side in enumerate(SIDES):

        @pl.when(exists(side))
        def _(index=index):
            copy(index).start()

    for t in range(side_cols // LANES):
        ext_ref[:, HALO // LANES + t, HALO : HALO + side_rows, :] = object_ref[
            :, :, t * LANES : (t + 1) * LANES
        ].astype(jnp.float32)
    spare = ext_ref.shape[1] - 1
    ext_ref[:, spare] = jnp.zeros((2, ext_ref.shape[2], LANES), jnp.float32)
    for index, side in enumerate(SIDES):
        dr, dc = opposite(side)
        rows = part(dr, HALO, side_rows)
        tiles = range(spare)[part(dc, HALO // LANES, side_cols // LANES)]

        @pl.when(exists((dr, dc)))
        def _(index=index, rows=rows, tiles=tiles):
            copy(index).wait_recv()
            for k, t in enumerate(tiles):
                ext_ref[:, t, rows, :] = landings[index][
                    :, :, k * LANES : (k + 1) * LANES
                ].astype(jnp.float32)

        @pl.when(jnp.logical_not(exists((dr, dc))))
        def _(rows=rows, tiles=tiles, index=index):
            for t in tiles:
                ext_ref[:, t, rows, :] = jnp.zeros(
                    (2, landings[index].shape[1], LANES), ext_ref.dtype
                )

    for index, side in enumerate(SIDES):

        @pl.when(exists(side))
        def _(index=index):
            copy(index).wait_send()


def halo_call(object_field):
    _, side_rows, side_cols = object_field.shape
    vmem = pl.BlockSpec(memory_space=pltpu.VMEM)
    landings = []
    for dr, dc in SIDES:
        landings.append(
            pltpu.VMEM((2, HALO if dr else side_rows, HALO if dc else side_cols), object_field.dtype)
        )
    sems = pltpu.SemaphoreType.DMA((len(SIDES),))
    return pl.pallas_call(
        halo_kernel,
        out_shape=jax.ShapeDtypeStruct(
            (2, (side_cols + 2 * HALO) // LANES + 1, side_rows + 2 * HALO, LANES), jnp.float32
        ),
        in_specs=[vmem],
        out_specs=vmem,
        scratch_shapes=landings + [sems, sems],
        compiler_params=pltpu.CompilerParams(
            collective_id=0, has_side_effects=True, vmem_limit_bytes=14 * 1024 * 1024
        ),
        name="halo",
    )(object_field)


def reduce_kernel(scale, acc_ref, pacc_ref, grad_ref, probe_ref, *scratch):
    count = len(SIDES)
    sends, landings, rest = scratch[:count], scratch[count : 2 * count], scratch[2 * count :]
    psend, pair_recv, merged, precv, zsend, zrecv, full = rest[:7]
    side_sems, pair_sems, col_sems, row_sems = rest[7:]
    row, col, n_row, n_col = position()
    side_rows, side_cols = grad_ref.shape[1:]
    margin = HALO // LANES
    inner = side_cols // LANES
    for index, (dr, dc) in enumerate(SIDES):
        tiles = range(inner + 2 * margin)[part(dc, margin, inner)]
        rows = part(dr, HALO, side_rows)
        for k, t in enumerate(tiles):
            sends[index][:, k] = acc_ref[:, t, rows, :].astype(jnp.bfloat16)
    psend[...] = pacc_ref[...].astype(jnp.bfloat16)

    barrier = pltpu.get_barrier_semaphore()
    waits = jnp.int32(n_row + n_col - 2)
    for k in range(1, n_col):
        pl.semaphore_signal(
            barrier, inc=1, device_id=(row, lax.rem(col + k, n_col)), device_id_type=MESH
        )
    for k in range(1, n_row):
        pl.semaphore_signal(
            barrier, inc=1, device_id=(lax.rem(row + k, n_row), col), device_id_type=MESH
        )
    for side in SIDES:
        if side[0] and side[1]:

            @pl.when(exists(side))
            def _(side=side):
                pl.semaphore_signal(barrier, inc=1, device_id=at_side(side), device_id_type=MESH)

            waits = waits + exists(side).astype(jnp.int32)
    pl.semaphore_wait(barrier, waits)

    share = psend.shape[0] // n_col
    piece = share // n_row
    chip, core = col // 2, lax.rem(col, 2)
    n_chip = n_col // 2
    sibling = (row, 2 * chip + 1 - core)

    def to_peer(source, landing, sems, which, k, device):
        return pltpu.make_async_remote_copy(
            src_ref=source,
            dst_ref=landing,
            send_sem=sems.at[which, k - 1],
            recv_sem=sems.at[which + 1, k - 1],
            device_id=device,
            device_id_type=MESH,
        )

    def chip_at(k):
        return lax.rem(chip + k, n_chip)

    def chip_from(k):
        return lax.rem(chip + n_chip - k, n_chip)

    def chip_peer(k):
        return (row, 2 * chip_at(k) + core)

    def row_peer(k):
        return (lax.rem(row + k, n_row), col)

    def share_of(ref, index):
        return ref.at[pl.ds(pl.multiple_of(index * share, share), share)]

    def pair_copy(k):
        source = share_of(psend, 2 * chip_at(k) + 1 - core)
        return to_peer(source, pair_recv.at[k], pair_sems, 0, k + 1, sibling)

    def scatter_copy(k):
        return to_peer(merged.at[k - 1], precv.at[k - 1], col_sems, 0, k, chip_peer(k))

    def row_scatter_copy(k):
        target = lax.rem(row + k, n_row)
        return to_peer(
            zsend.at[pl.ds(pl.multiple_of(target * piece, piece), piece)],
            zrecv.at[k - 1],
            row_sems,
            0,
            k,
            row_peer(k),
        )

    def piece_of(index):
        start = pl.multiple_of(col * share + index * piece, piece)
        return full.at[pl.ds(start, piece)]

    def row_gather_copy(k, owner):
        return to_peer(piece_of(row), piece_of(owner), row_sems, 2, k, row_peer(k))

    def gather_copy(k, owner):
        return to_peer(share_of(full, col), share_of(full, owner), col_sems, 2, k, chip_peer(k))

    def forward_copy(k, side):
        source = share_of(full, 2 * chip_from(k) + core)
        landing = share_of(full, 2 * chip_from(k) + side)
        return to_peer(source, landing, pair_sems, 2, k + 1, sibling)

    def side_copy(index):
        return to_side(
            SIDES[index], index, sends[index], landings[index], side_sems.at[0], side_sems.at[1]
        )

    order = list(range(1, n_chip)) + [0]
    for k in order:
        pair_copy(k).start()

    def start_sides(chosen):
        for index, side in enumerate(SIDES):
            if chosen(side):

                @pl.when(exists(side))
                def _(index=index):
                    side_copy(index).start()

    start_sides(lambda side: side[1] == 0)
    def merge(k):
        pair_copy(k).wait_recv()
        index = 2 * chip_at(k) + core
        own = pacc_ref[pl.ds(pl.multiple_of(index * share, share), share), :]
        return own + pair_recv[k].astype(jnp.float32)

    for k in range(1, n_chip):
        merged[k - 1] = merge(k).astype(jnp.bfloat16)
        scatter_copy(k).start()
    total = merge(0)
    for t in range(inner):
        grad_ref[:, :, t * LANES : (t + 1) * LANES] = acc_ref[
            :, margin + t, HALO : HALO + side_rows, :
        ]
    for k in range(1, n_chip):
        scatter_copy(k).wait_recv()
        total = total + precv[k - 1].astype(jnp.float32)
    zsend[...] = total
    for k in range(1, n_row):
        row_scatter_copy(k).start()
    start_sides(lambda side: side[0] == 0)
    start_sides(lambda side: side[0] != 0 and side[1] != 0)
    own = zsend[pl.ds(pl.multiple_of(row * piece, piece), piece), :]
    for k in range(1, n_row):
        row_scatter_copy(k).wait_recv()
        own = own + zrecv[k - 1]
    start = pl.multiple_of(col * share + row * piece, piece)
    full[pl.ds(start, piece), :] = (own * scale).astype(jnp.bfloat16)
    for k in range(1, n_row):
        row_gather_copy(k, row).start()
    for k in range(1, n_row):
        row_gather_copy(k, lax.rem(row + n_row - k, n_row)).wait_recv()
    for k in range(1, n_chip):
        gather_copy(k, col).start()
    forward_copy(0, core).start()
    for k in range(1, n_chip):
        gather_copy(k, 2 * chip_from(k) + core).wait_recv()
        forward_copy(k, core).start()

    for index, side in enumerate(SIDES):
        dr, dc = opposite(side)
        rows = edge(dr, HALO, side_rows)
        tiles = range(inner)[edge(dc, margin, inner)]

        @pl.when(exists((dr, dc)))
        def _(index=index, rows=rows, tiles=tiles):
            side_copy(index).wait_recv()
            for k, t in enumerate(tiles):
                grad_ref[:, rows, t * LANES : (t + 1) * LANES] += landings[index][:, k].astype(
                    jnp.float32
                )

    for k in range(n_chip):
        forward_copy(k, 1 - core).wait_recv()
    parts, modes, fs, width = probe_ref.shape
    at = 0
    for p in range(parts):
        for m in range(modes):
            for t in range(width // LANES):
                probe_ref[p, m, :, t * LANES : (t + 1) * LANES] = full[at : at + fs, :].astype(
                    jnp.float32
                )
                at += fs
    for k in range(1, n_chip):
        scatter_copy(k).wait_send()
        gather_copy(k, col).wait_send()
    for k in range(n_chip):
        pair_copy(k).wait_send()
        forward_copy(k, core).wait_send()
    for k in range(1, n_row):
        row_scatter_copy(k).wait_send()
        row_gather_copy(k, row).wait_send()
    for index, side in enumerate(SIDES):

        @pl.when(exists(side))
        def _(index=index):
            side_copy(index).wait_send()


def reduce_call(acc, probe_flat, object_shape, probe_shape, scale):
    n_row, n_col = lax.axis_size("row"), lax.axis_size("col")
    _, side_rows, side_cols = object_shape
    inner = side_cols // LANES
    margin = HALO // LANES
    vmem = pl.BlockSpec(memory_space=pltpu.VMEM)
    buffers = []
    for dr, dc in SIDES:
        buffers.append(
            pltpu.VMEM(
                (2, margin if dc else inner, HALO if dr else side_rows, LANES), jnp.bfloat16
            )
        )
    total_rows = probe_flat.shape[0]
    share = total_rows // n_col
    piece = share // n_row
    n_chip = n_col // 2
    return pl.pallas_call(
        functools.partial(reduce_kernel, scale),
        out_shape=(
            jax.ShapeDtypeStruct(object_shape, jnp.float32),
            jax.ShapeDtypeStruct(probe_shape, jnp.float32),
        ),
        in_specs=[vmem, vmem],
        out_specs=(vmem, vmem),
        scratch_shapes=buffers
        + buffers
        + [
            pltpu.VMEM((total_rows, LANES), jnp.bfloat16),
            pltpu.VMEM((n_chip, share, LANES), jnp.bfloat16),
            pltpu.VMEM((n_chip - 1, share, LANES), jnp.bfloat16),
            pltpu.VMEM((n_chip - 1, share, LANES), jnp.bfloat16),
            pltpu.VMEM((share, LANES), jnp.float32),
            pltpu.VMEM((n_row - 1, piece, LANES), jnp.float32),
            pltpu.VMEM((total_rows, LANES), jnp.bfloat16),
            pltpu.SemaphoreType.DMA((2, len(SIDES))),
            pltpu.SemaphoreType.DMA((4, n_chip)),
            pltpu.SemaphoreType.DMA((4, n_chip - 1)),
            pltpu.SemaphoreType.DMA((4, n_row - 1)),
        ],
        compiler_params=pltpu.CompilerParams(
            collective_id=1, has_side_effects=True, vmem_limit_bytes=20 * 1024 * 1024
        ),
        name="reduce",
    )(acc, probe_flat)


def fourier_tables(frame_side):
    indices = np.arange(frame_side)
    product = indices[:, None] * indices[None, :] % frame_side
    angles = 2.0 * math.pi / frame_side * product
    norm_scale = 1.0 / math.sqrt(frame_side)
    return (
        jnp.asarray((np.cos(angles) * norm_scale).astype(np.float32)).astype(jnp.bfloat16),
        jnp.asarray((-np.sin(angles) * norm_scale).astype(np.float32)).astype(jnp.bfloat16),
    )


CHUNK = 32


def dot32(left, right):
    return jnp.dot(left, right, preferred_element_type=jnp.float32)


def frames_kernel(
    count_ref, at_ref, ext_ref, probe_ref, amp_ref, tr_ref, ti_ref, acc_ref, pacc_ref,
    fwd, inv, *buffers,
):
    fs = probe_ref.shape[-1]
    modes = probe_ref.shape[1]
    lane_tiles = fs // LANES
    last_slot = amp_ref.shape[0] - 1
    live = count_ref[0]
    even, odd = buffers[:4], buffers[4:]
    acc_ref[...] = jnp.zeros(acc_ref.shape, jnp.float32)
    pacc_ref[...] = jnp.zeros(pacc_ref.shape, jnp.float32)
    odd[2][...] = jnp.zeros(odd[2].shape, jnp.float32)
    odd[3][...] = jnp.zeros(odd[3].shape, jnp.float32)
    table_real, table_imag = tr_ref[...], ti_ref[...]
    minus = -table_imag
    fwd[:fs, :fs] = table_real
    fwd[:fs, fs:] = minus
    fwd[fs:, :fs] = table_imag
    fwd[fs:, fs:] = table_real
    inv[:fs, :fs] = table_real
    inv[:fs, fs:] = table_imag
    inv[fs:, :fs] = minus
    inv[fs:, fs:] = table_real

    def two_sided(buffer, left_table, right_table):
        stage, half, wide, _ = buffer
        for m in range(modes):
            both = dot32(left_table[...], stage[:, m * fs : (m + 1) * fs])
            half[m * fs : (m + 1) * fs, :fs] = both[:fs].astype(jnp.bfloat16)
            half[m * fs : (m + 1) * fs, fs:] = both[fs:].astype(jnp.bfloat16)
        wide[...] = dot32(half[...], right_table[...])

    def make_exit(buffer, slot):
        stage, _, _, patch = buffer
        row_at = at_ref[0, slot]
        col_at = at_ref[1, slot]
        tile_at = col_at // LANES
        shift = col_at % LANES
        back_shift = (LANES - shift) % LANES
        lane = lax.broadcasted_iota(jnp.int32, (CHUNK, LANES), 1)
        keep_low = lane < LANES - shift
        for r in range(0, fs, CHUNK):
            rows = slice(r, r + CHUNK)
            values = []
            for plane in range(2):
                rolled = [
                    pltpu.roll(
                        ext_ref[plane, tile_at + t, pl.ds(row_at + r, CHUNK), :], back_shift, 1
                    )
                    for t in range(lane_tiles + 1)
                ]
                values.append(
                    [jnp.where(keep_low, rolled[t], rolled[t + 1]) for t in range(lane_tiles)]
                )
            for t in range(lane_tiles):
                cols = slice(t * LANES, (t + 1) * LANES)
                patch_real, patch_imag = values[0][t], values[1][t]
                patch[0, rows, cols] = patch_real
                patch[1, rows, cols] = patch_imag
                for m in range(modes):
                    probe_real = probe_ref[0, m, rows, cols]
                    probe_imag = probe_ref[1, m, rows, cols]
                    out = slice(m * fs + t * LANES, m * fs + (t + 1) * LANES)
                    stage[rows, out] = (
                        probe_real * patch_real - probe_imag * patch_imag
                    ).astype(jnp.bfloat16)
                    stage[fs + r : fs + r + CHUNK, out] = (
                        probe_real * patch_imag + probe_imag * patch_real
                    ).astype(jnp.bfloat16)

    def make_chi(buffer, slot, valid):
        stage, _, wide, _ = buffer
        for r in range(0, fs, CHUNK):
            for t in range(lane_tiles):
                cols = slice(t * LANES, (t + 1) * LANES)
                imag_cols = slice(fs + t * LANES, fs + (t + 1) * LANES)
                psi = []
                power = None
                for m in range(modes):
                    rows = slice(m * fs + r, m * fs + r + CHUNK)
                    real, imag = wide[rows, cols], wide[rows, imag_cols]
                    psi.append((real, imag))
                    own = real * real + imag * imag
                    power = own if power is None else power + own
                amp = amp_ref[slot, r : r + CHUNK, cols].astype(jnp.float32)
                factor = 1.0 - amp * lax.rsqrt(jnp.maximum(power, 0.25))
                if valid is not None:
                    factor = jnp.where(valid, factor, 0.0)
                for m in range(modes):
                    out = slice(m * fs + t * LANES, m * fs + (t + 1) * LANES)
                    stage[r : r + CHUNK, out] = (psi[m][0] * factor).astype(jnp.bfloat16)
                    stage[fs + r : fs + r + CHUNK, out] = (psi[m][1] * factor).astype(jnp.bfloat16)

    def add_grads(buffer, slot):
        _, _, wide, patch = buffer
        row_at = at_ref[0, slot]
        col_at = at_ref[1, slot]
        tile_at = col_at // LANES
        shift = col_at % LANES
        lane = lax.broadcasted_iota(jnp.int32, (CHUNK, LANES), 1)
        from_same = lane >= shift
        for r in range(0, fs, CHUNK):
            grads = [[], []]
            for t in range(lane_tiles):
                cols = slice(t * LANES, (t + 1) * LANES)
                imag_cols = slice(fs + t * LANES, fs + (t + 1) * LANES)
                patch_real = patch[0, r : r + CHUNK, cols]
                patch_imag = patch[1, r : r + CHUNK, cols]
                total_real = total_imag = None
                for m in range(modes):
                    rows = slice(m * fs + r, m * fs + r + CHUNK)
                    real, imag = wide[rows, cols], wide[rows, imag_cols]
                    probe_real = probe_ref[0, m, r : r + CHUNK, cols]
                    probe_imag = probe_ref[1, m, r : r + CHUNK, cols]
                    own_real = probe_real * real + probe_imag * imag
                    own_imag = probe_real * imag - probe_imag * real
                    total_real = own_real if m == 0 else total_real + own_real
                    total_imag = own_imag if m == 0 else total_imag + own_imag
                    at = (m * lane_tiles + t) * fs + r
                    pacc_ref[at : at + CHUNK, :] += patch_real * real + patch_imag * imag
                    at += modes * lane_tiles * fs
                    pacc_ref[at : at + CHUNK, :] += patch_real * imag - patch_imag * real
                grads[0].append(pltpu.roll(total_real, shift, 1))
                grads[1].append(pltpu.roll(total_imag, shift, 1))
            for plane in range(2):
                rolled = grads[plane]
                for t in range(lane_tiles + 1):
                    same = rolled[t] if t < lane_tiles else 0.0
                    before = rolled[t - 1] if t > 0 else 0.0
                    where = (plane, tile_at + t, pl.ds(row_at + r, CHUNK), slice(None))
                    acc_ref[where] += jnp.where(from_same, same, before)

    def advance(pair, carry):
        first = 2 * pair
        second = jnp.minimum(first + 1, last_slot)
        make_exit(even, first)
        two_sided(even, fwd, inv)
        add_grads(odd, jnp.maximum(first - 1, 0))
        make_exit(odd, second)
        two_sided(odd, fwd, inv)
        make_chi(even, first, None)
        two_sided(even, inv, fwd)
        make_chi(odd, second, first + 1 < live)
        two_sided(odd, inv, fwd)
        add_grads(even, first)
        return carry

    pairs = (live + 1) // 2
    lax.fori_loop(0, pairs, advance, 0)
    add_grads(odd, jnp.minimum(2 * pairs - 1, last_slot))


def frames_call(extended, probe_modes, amplitudes, positions, live_count, tables):
    fs = probe_modes.shape[-1]
    modes = probe_modes.shape[1]
    tiled = extended.shape
    vmem = pl.BlockSpec(memory_space=pltpu.VMEM)
    smem = pl.BlockSpec(memory_space=pltpu.SMEM)
    return pl.pallas_call(
        frames_kernel,
        out_shape=(
            jax.ShapeDtypeStruct(tiled, jnp.float32),
            jax.ShapeDtypeStruct((probe_modes.size // LANES, LANES), jnp.float32),
        ),
        in_specs=[smem, smem, vmem, vmem, vmem, vmem, vmem],
        out_specs=(vmem, vmem),
        scratch_shapes=[
            pltpu.VMEM((2 * fs, 2 * fs), jnp.bfloat16),
            pltpu.VMEM((2 * fs, 2 * fs), jnp.bfloat16),
        ]
        + 2
        * [
            pltpu.VMEM((2 * fs, modes * fs), jnp.bfloat16),
            pltpu.VMEM((modes * fs, 2 * fs), jnp.bfloat16),
            pltpu.VMEM((modes * fs, 2 * fs), jnp.float32),
            pltpu.VMEM((2, fs, fs), jnp.float32),
        ],
        compiler_params=pltpu.CompilerParams(vmem_limit_bytes=26 * 1024 * 1024),
        name="frames",
    )(live_count.reshape(1), positions, extended, probe_modes, amplitudes, *tables)


def shards(object_field, probe_modes, measured_amp, scan_positions, frame_counts):
    slot_count = measured_amp.shape[2]
    extended = halo_call(object_field)
    acc, probe_flat = frames_call(
        extended,
        probe_modes,
        measured_amp[0, 0],
        scan_positions[0, 0],
        frame_counts[0, 0],
        fourier_tables(probe_modes.shape[-1]),
    )
    norm_scale = 1.0 / math.sqrt(lax.axis_size("row") * lax.axis_size("col") * slot_count)
    return reduce_call(acc, probe_flat, object_field.shape, probe_modes.shape, norm_scale)


def solution(mesh):
    in_specs = (
        P(None, "row", "col"),
        P(),
        P("row", "col", None, None, None),
        P("row", "col", None, None),
        P("row", "col"),
    )
    out_specs = (P(None, "row", "col"), P())
    return jax.shard_map(shards, mesh=mesh, in_specs=in_specs, out_specs=out_specs, check_vma=False)
```

```python
import functools
import math

import jax
import jax.numpy as jnp
import numpy as np
from jax import lax
from jax.experimental import pallas as pl
from jax.experimental.pallas import tpu as pltpu
from jax.sharding import PartitionSpec as P

HALO = 128
LANES = 128


MESH = pl.DeviceIdType.MESH
SIDES = [(dr, dc) for dr in (-1, 0, 1) for dc in (-1, 0, 1) if (dr, dc) != (0, 0)]


def position():
    return (
        lax.axis_index("row"),
        lax.axis_index("col"),
        lax.axis_size("row"),
        lax.axis_size("col"),
    )


def exists(side):
    row, col, rows, cols = position()
    dr, dc = side
    inside = jnp.bool_(True)
    if dr:
        inside = row + dr >= 0 if dr < 0 else row + dr < rows
    if dc:
        other = col + dc >= 0 if dc < 0 else col + dc < cols
        inside = jnp.logical_and(inside, other) if dr else other
    return inside


def at_side(side):
    row, col, _, _ = position()
    return (row + side[0], col + side[1])


def opposite(side):
    return (-side[0], -side[1])


def part(step, margin, inner):
    return {-1: slice(0, margin), 0: slice(margin, margin + inner), 1: slice(margin + inner, None)}[
        step
    ]


def edge(step, margin, inner):
    return {-1: slice(0, margin), 0: slice(0, inner), 1: slice(inner - margin, inner)}[step]


def to_side(side, index, source, landing, send_sems, recv_sems):
    return pltpu.make_async_remote_copy(
        src_ref=source,
        dst_ref=landing,
        send_sem=send_sems.at[index],
        recv_sem=recv_sems.at[index],
        device_id=at_side(side),
        device_id_type=MESH,
    )


def halo_kernel(whole_ref, ext_ref, *scratch):
    landings, (send_sems, recv_sems) = scratch[: len(SIDES)], scratch[len(SIDES) : -2]
    object_ref, load_sem = scratch[-2:]
    load = pltpu.make_async_copy(whole_ref, object_ref, load_sem)
    load.start()
    side_rows, side_cols = object_ref.shape[1:]
    barrier = pltpu.get_barrier_semaphore()
    count = jnp.int32(0)
    for side in SIDES:

        @pl.when(exists(side))
        def _(side=side):
            pl.semaphore_signal(barrier, inc=1, device_id=at_side(side), device_id_type=MESH)

        count = count + exists(side).astype(jnp.int32)
    pl.semaphore_wait(barrier, count)
    load.wait()

    def copy(index):
        dr, dc = SIDES[index]
        source = object_ref.at[:, edge(dr, HALO, side_rows), edge(dc, HALO, side_cols)]
        return to_side(SIDES[index], index, source, landings[index], send_sems, recv_sems)

    for index, side in enumerate(SIDES):

        @pl.when(exists(side))
        def _(index=index):
            copy(index).start()

    for t in range(side_cols // LANES):
        ext_ref[:, HALO // LANES + t, HALO : HALO + side_rows, :] = object_ref[
            :, :, t * LANES : (t + 1) * LANES
        ].astype(jnp.float32)
    spare = ext_ref.shape[1] - 1
    ext_ref[:, spare] = jnp.zeros((2, ext_ref.shape[2], LANES), jnp.float32)
    for index, side in enumerate(SIDES):
        dr, dc = opposite(side)
        rows = part(dr, HALO, side_rows)
        tiles = range(spare)[part(dc, HALO // LANES, side_cols // LANES)]

        @pl.when(exists((dr, dc)))
        def _(index=index, rows=rows, tiles=tiles):
            copy(index).wait_recv()
            for k, t in enumerate(tiles):
                ext_ref[:, t, rows, :] = landings[index][
                    :, :, k * LANES : (k + 1) * LANES
                ].astype(jnp.float32)

        @pl.when(jnp.logical_not(exists((dr, dc))))
        def _(rows=rows, tiles=tiles, index=index):
            for t in tiles:
                ext_ref[:, t, rows, :] = jnp.zeros(
                    (2, landings[index].shape[1], LANES), ext_ref.dtype
                )

    for index, side in enumerate(SIDES):

        @pl.when(exists(side))
        def _(index=index):
            copy(index).wait_send()


def halo_call(object_field):
    _, side_rows, side_cols = object_field.shape
    vmem = pl.BlockSpec(memory_space=pltpu.VMEM)
    landings = []
    for dr, dc in SIDES:
        landings.append(
            pltpu.VMEM((2, HALO if dr else side_rows, HALO if dc else side_cols), object_field.dtype)
        )
    sems = pltpu.SemaphoreType.DMA((len(SIDES),))
    return pl.pallas_call(
        halo_kernel,
        out_shape=jax.ShapeDtypeStruct(
            (2, (side_cols + 2 * HALO) // LANES + 1, side_rows + 2 * HALO, LANES), jnp.float32
        ),
        in_specs=[pl.BlockSpec(memory_space=pltpu.HBM)],
        out_specs=vmem,
        scratch_shapes=landings
        + [sems, sems, pltpu.VMEM(object_field.shape, object_field.dtype), pltpu.SemaphoreType.DMA],
        compiler_params=pltpu.CompilerParams(
            collective_id=0, has_side_effects=True, vmem_limit_bytes=14 * 1024 * 1024
        ),
        name="halo",
    )(object_field)


def reduce_kernel(scale, acc_ref, pacc_ref, grad_ref, probe_ref, *scratch):
    count = len(SIDES)
    sends, landings, rest = scratch[:count], scratch[count : 2 * count], scratch[2 * count :]
    psend, pair_recv, merged, precv, zsend, zrecv, full = rest[:7]
    side_sems, pair_sems, col_sems, row_sems = rest[7:]
    row, col, n_row, n_col = position()
    side_rows, side_cols = grad_ref.shape[1:]
    margin = HALO // LANES
    inner = side_cols // LANES
    for index, (dr, dc) in enumerate(SIDES):
        tiles = range(inner + 2 * margin)[part(dc, margin, inner)]
        rows = part(dr, HALO, side_rows)
        for k, t in enumerate(tiles):
            sends[index][:, k] = acc_ref[:, t, rows, :].astype(jnp.bfloat16)
    psend[...] = pacc_ref[...].astype(jnp.bfloat16)

    barrier = pltpu.get_barrier_semaphore()
    waits = jnp.int32(n_row + n_col - 2)
    for k in range(1, n_col):
        pl.semaphore_signal(
            barrier, inc=1, device_id=(row, lax.rem(col + k, n_col)), device_id_type=MESH
        )
    for k in range(1, n_row):
        pl.semaphore_signal(
            barrier, inc=1, device_id=(lax.rem(row + k, n_row), col), device_id_type=MESH
        )
    for side in SIDES:
        if side[0] and side[1]:

            @pl.when(exists(side))
            def _(side=side):
                pl.semaphore_signal(barrier, inc=1, device_id=at_side(side), device_id_type=MESH)

            waits = waits + exists(side).astype(jnp.int32)
    pl.semaphore_wait(barrier, waits)

    share = psend.shape[0] // n_col
    piece = share // n_row
    chip, core = col // 2, lax.rem(col, 2)
    n_chip = n_col // 2
    sibling = (row, 2 * chip + 1 - core)

    def to_peer(source, landing, sems, which, k, device):
        return pltpu.make_async_remote_copy(
            src_ref=source,
            dst_ref=landing,
            send_sem=sems.at[which, k - 1],
            recv_sem=sems.at[which + 1, k - 1],
            device_id=device,
            device_id_type=MESH,
        )

    def chip_at(k):
        return lax.rem(chip + k, n_chip)

    def chip_from(k):
        return lax.rem(chip + n_chip - k, n_chip)

    def chip_peer(k):
        return (row, 2 * chip_at(k) + core)

    def row_peer(k):
        return (lax.rem(row + k, n_row), col)

    def share_of(ref, index):
        return ref.at[pl.ds(pl.multiple_of(index * share, share), share)]

    def pair_copy(k):
        source = share_of(psend, 2 * chip_at(k) + 1 - core)
        return to_peer(source, pair_recv.at[k], pair_sems, 0, k + 1, sibling)

    def scatter_copy(k):
        return to_peer(merged.at[k - 1], precv.at[k - 1], col_sems, 0, k, chip_peer(k))

    def row_scatter_copy(k):
        target = lax.rem(row + k, n_row)
        return to_peer(
            zsend.at[pl.ds(pl.multiple_of(target * piece, piece), piece)],
            zrecv.at[k - 1],
            row_sems,
            0,
            k,
            row_peer(k),
        )

    def piece_of(index):
        start = pl.multiple_of(col * share + index * piece, piece)
        return full.at[pl.ds(start, piece)]

    def row_gather_copy(k, owner):
        return to_peer(piece_of(row), piece_of(owner), row_sems, 2, k, row_peer(k))

    def gather_copy(k, owner):
        return to_peer(share_of(full, col), share_of(full, owner), col_sems, 2, k, chip_peer(k))

    def forward_copy(k, side):
        source = share_of(full, 2 * chip_from(k) + core)
        landing = share_of(full, 2 * chip_from(k) + side)
        return to_peer(source, landing, pair_sems, 2, k + 1, sibling)

    def side_copy(index):
        return to_side(
            SIDES[index], index, sends[index], landings[index], side_sems.at[0], side_sems.at[1]
        )

    order = list(range(1, n_chip)) + [0]
    for k in order:
        pair_copy(k).start()

    def start_sides(chosen):
        for index, side in enumerate(SIDES):
            if chosen(side):

                @pl.when(exists(side))
                def _(index=index):
                    side_copy(index).start()

    start_sides(lambda side: side[1] == 0)
    def merge(k):
        pair_copy(k).wait_recv()
        index = 2 * chip_at(k) + core
        own = pacc_ref[pl.ds(pl.multiple_of(index * share, share), share), :]
        return own + pair_recv[k].astype(jnp.float32)

    for k in range(1, n_chip):
        merged[k - 1] = merge(k).astype(jnp.bfloat16)
        scatter_copy(k).start()
    total = merge(0)
    for t in range(inner):
        grad_ref[:, :, t * LANES : (t + 1) * LANES] = acc_ref[
            :, margin + t, HALO : HALO + side_rows, :
        ]
    for k in range(1, n_chip):
        scatter_copy(k).wait_recv()
        total = total + precv[k - 1].astype(jnp.float32)
    zsend[...] = total
    for k in range(1, n_row):
        row_scatter_copy(k).start()
    start_sides(lambda side: side[0] == 0)
    start_sides(lambda side: side[0] != 0 and side[1] != 0)
    own = zsend[pl.ds(pl.multiple_of(row * piece, piece), piece), :]
    for k in range(1, n_row):
        row_scatter_copy(k).wait_recv()
        own = own + zrecv[k - 1]
    start = pl.multiple_of(col * share + row * piece, piece)
    full[pl.ds(start, piece), :] = (own * scale).astype(jnp.bfloat16)
    for k in range(1, n_row):
        row_gather_copy(k, row).start()
    for k in range(1, n_row):
        row_gather_copy(k, lax.rem(row + n_row - k, n_row)).wait_recv()
    for k in range(1, n_chip):
        gather_copy(k, col).start()
    forward_copy(0, core).start()
    for k in range(1, n_chip):
        gather_copy(k, 2 * chip_from(k) + core).wait_recv()
        forward_copy(k, core).start()

    for index, side in enumerate(SIDES):
        dr, dc = opposite(side)
        rows = edge(dr, HALO, side_rows)
        tiles = range(inner)[edge(dc, margin, inner)]

        @pl.when(exists((dr, dc)))
        def _(index=index, rows=rows, tiles=tiles):
            side_copy(index).wait_recv()
            for k, t in enumerate(tiles):
                grad_ref[:, rows, t * LANES : (t + 1) * LANES] += landings[index][:, k].astype(
                    jnp.float32
                )

    for k in range(n_chip):
        forward_copy(k, 1 - core).wait_recv()
    parts, modes, fs, width = probe_ref.shape
    at = 0
    for p in range(parts):
        for m in range(modes):
            for t in range(width // LANES):
                probe_ref[p, m, :, t * LANES : (t + 1) * LANES] = full[at : at + fs, :].astype(
                    jnp.float32
                )
                at += fs
    for k in range(1, n_chip):
        scatter_copy(k).wait_send()
        gather_copy(k, col).wait_send()
    for k in range(n_chip):
        pair_copy(k).wait_send()
        forward_copy(k, core).wait_send()
    for k in range(1, n_row):
        row_scatter_copy(k).wait_send()
        row_gather_copy(k, row).wait_send()
    for index, side in enumerate(SIDES):

        @pl.when(exists(side))
        def _(index=index):
            side_copy(index).wait_send()


def reduce_call(acc, probe_flat, object_shape, probe_shape, scale):
    n_row, n_col = lax.axis_size("row"), lax.axis_size("col")
    _, side_rows, side_cols = object_shape
    inner = side_cols // LANES
    margin = HALO // LANES
    vmem = pl.BlockSpec(memory_space=pltpu.VMEM)
    buffers = []
    for dr, dc in SIDES:
        buffers.append(
            pltpu.VMEM(
                (2, margin if dc else inner, HALO if dr else side_rows, LANES), jnp.bfloat16
            )
        )
    total_rows = probe_flat.shape[0]
    share = total_rows // n_col
    piece = share // n_row
    n_chip = n_col // 2
    return pl.pallas_call(
        functools.partial(reduce_kernel, scale),
        out_shape=(
            jax.ShapeDtypeStruct(object_shape, jnp.float32),
            jax.ShapeDtypeStruct(probe_shape, jnp.float32),
        ),
        in_specs=[vmem, vmem],
        out_specs=(vmem, vmem),
        scratch_shapes=buffers
        + buffers
        + [
            pltpu.VMEM((total_rows, LANES), jnp.bfloat16),
            pltpu.VMEM((n_chip, share, LANES), jnp.bfloat16),
            pltpu.VMEM((n_chip - 1, share, LANES), jnp.bfloat16),
            pltpu.VMEM((n_chip - 1, share, LANES), jnp.bfloat16),
            pltpu.VMEM((share, LANES), jnp.float32),
            pltpu.VMEM((n_row - 1, piece, LANES), jnp.float32),
            pltpu.VMEM((total_rows, LANES), jnp.bfloat16),
            pltpu.SemaphoreType.DMA((2, len(SIDES))),
            pltpu.SemaphoreType.DMA((4, n_chip)),
            pltpu.SemaphoreType.DMA((4, n_chip - 1)),
            pltpu.SemaphoreType.DMA((4, n_row - 1)),
        ],
        compiler_params=pltpu.CompilerParams(
            collective_id=1, has_side_effects=True, vmem_limit_bytes=20 * 1024 * 1024
        ),
        name="reduce",
    )(acc, probe_flat)


def fourier_tables(frame_side):
    indices = np.arange(frame_side)
    product = indices[:, None] * indices[None, :] % frame_side
    angles = 2.0 * math.pi / frame_side * product
    norm_scale = 1.0 / math.sqrt(frame_side)
    return (
        jnp.asarray((np.cos(angles) * norm_scale).astype(np.float32)).astype(jnp.bfloat16),
        jnp.asarray((-np.sin(angles) * norm_scale).astype(np.float32)).astype(jnp.bfloat16),
    )


CHUNK = 32


def dot32(left, right):
    return jnp.dot(left, right, preferred_element_type=jnp.float32)


def frames_kernel(
    count_ref, at_ref, ext_ref, probe_ref, amp_ref, tr_ref, ti_ref, acc_ref, pacc_ref,
    fwd, inv, *buffers,
):
    fs = probe_ref.shape[-1]
    modes = probe_ref.shape[1]
    lane_tiles = fs // LANES
    last_slot = amp_ref.shape[0] - 1
    live = count_ref[0]
    even, odd = buffers[:4], buffers[4:]
    acc_ref[...] = jnp.zeros(acc_ref.shape, jnp.float32)
    pacc_ref[...] = jnp.zeros(pacc_ref.shape, jnp.float32)
    odd[2][...] = jnp.zeros(odd[2].shape, jnp.float32)
    odd[3][...] = jnp.zeros(odd[3].shape, jnp.float32)
    table_real, table_imag = tr_ref[...], ti_ref[...]
    minus = -table_imag
    fwd[:fs, :fs] = table_real
    fwd[:fs, fs:] = minus
    fwd[fs:, :fs] = table_imag
    fwd[fs:, fs:] = table_real
    inv[:fs, :fs] = table_real
    inv[:fs, fs:] = table_imag
    inv[fs:, :fs] = minus
    inv[fs:, fs:] = table_real

    def two_sided(buffer, left_table, right_table):
        stage, half, wide, _ = buffer
        for m in range(modes):
            both = dot32(left_table[...], stage[:, m * fs : (m + 1) * fs])
            half[m * fs : (m + 1) * fs, :fs] = both[:fs].astype(jnp.bfloat16)
            half[m * fs : (m + 1) * fs, fs:] = both[fs:].astype(jnp.bfloat16)
        wide[...] = dot32(half[...], right_table[...])

    def make_exit(buffer, slot):
        stage, _, _, patch = buffer
        row_at = at_ref[0, slot]
        col_at = at_ref[1, slot]
        tile_at = col_at // LANES
        shift = col_at % LANES
        back_shift = (LANES - shift) % LANES
        lane = lax.broadcasted_iota(jnp.int32, (CHUNK, LANES), 1)
        keep_low = lane < LANES - shift
        for r in range(0, fs, CHUNK):
            rows = slice(r, r + CHUNK)
            values = []
            for plane in range(2):
                rolled = [
                    pltpu.roll(
                        ext_ref[plane, tile_at + t, pl.ds(row_at + r, CHUNK), :], back_shift, 1
                    )
                    for t in range(lane_tiles + 1)
                ]
                values.append(
                    [jnp.where(keep_low, rolled[t], rolled[t + 1]) for t in range(lane_tiles)]
                )
            for t in range(lane_tiles):
                cols = slice(t * LANES, (t + 1) * LANES)
                patch_real, patch_imag = values[0][t], values[1][t]
                patch[0, rows, cols] = patch_real
                patch[1, rows, cols] = patch_imag
                for m in range(modes):
                    probe_real = probe_ref[0, m, rows, cols]
                    probe_imag = probe_ref[1, m, rows, cols]
                    out = slice(m * fs + t * LANES, m * fs + (t + 1) * LANES)
                    stage[rows, out] = (
                        probe_real * patch_real - probe_imag * patch_imag
                    ).astype(jnp.bfloat16)
                    stage[fs + r : fs + r + CHUNK, out] = (
                        probe_real * patch_imag + probe_imag * patch_real
                    ).astype(jnp.bfloat16)

    def make_chi(buffer, slot, valid):
        stage, _, wide, _ = buffer
        for r in range(0, fs, CHUNK):
            for t in range(lane_tiles):
                cols = slice(t * LANES, (t + 1) * LANES)
                imag_cols = slice(fs + t * LANES, fs + (t + 1) * LANES)
                psi = []
                power = None
                for m in range(modes):
                    rows = slice(m * fs + r, m * fs + r + CHUNK)
                    real, imag = wide[rows, cols], wide[rows, imag_cols]
                    psi.append((real, imag))
                    own = real * real + imag * imag
                    power = own if power is None else power + own
                amp = amp_ref[slot, r : r + CHUNK, cols].astype(jnp.float32)
                factor = 1.0 - amp * lax.rsqrt(jnp.maximum(power, 0.25))
                if valid is not None:
                    factor = jnp.where(valid, factor, 0.0)
                for m in range(modes):
                    out = slice(m * fs + t * LANES, m * fs + (t + 1) * LANES)
                    stage[r : r + CHUNK, out] = (psi[m][0] * factor).astype(jnp.bfloat16)
                    stage[fs + r : fs + r + CHUNK, out] = (psi[m][1] * factor).astype(jnp.bfloat16)

    def add_grads(buffer, slot):
        _, _, wide, patch = buffer
        row_at = at_ref[0, slot]
        col_at = at_ref[1, slot]
        tile_at = col_at // LANES
        shift = col_at % LANES
        lane = lax.broadcasted_iota(jnp.int32, (CHUNK, LANES), 1)
        from_same = lane >= shift
        for r in range(0, fs, CHUNK):
            grads = [[], []]
            for t in range(lane_tiles):
                cols = slice(t * LANES, (t + 1) * LANES)
                imag_cols = slice(fs + t * LANES, fs + (t + 1) * LANES)
                patch_real = patch[0, r : r + CHUNK, cols]
                patch_imag = patch[1, r : r + CHUNK, cols]
                total_real = total_imag = None
                for m in range(modes):
                    rows = slice(m * fs + r, m * fs + r + CHUNK)
                    real, imag = wide[rows, cols], wide[rows, imag_cols]
                    probe_real = probe_ref[0, m, r : r + CHUNK, cols]
                    probe_imag = probe_ref[1, m, r : r + CHUNK, cols]
                    own_real = probe_real * real + probe_imag * imag
                    own_imag = probe_real * imag - probe_imag * real
                    total_real = own_real if m == 0 else total_real + own_real
                    total_imag = own_imag if m == 0 else total_imag + own_imag
                    at = (m * lane_tiles + t) * fs + r
                    pacc_ref[at : at + CHUNK, :] += patch_real * real + patch_imag * imag
                    at += modes * lane_tiles * fs
                    pacc_ref[at : at + CHUNK, :] += patch_real * imag - patch_imag * real
                grads[0].append(pltpu.roll(total_real, shift, 1))
                grads[1].append(pltpu.roll(total_imag, shift, 1))
            for plane in range(2):
                rolled = grads[plane]
                for t in range(lane_tiles + 1):
                    same = rolled[t] if t < lane_tiles else 0.0
                    before = rolled[t - 1] if t > 0 else 0.0
                    where = (plane, tile_at + t, pl.ds(row_at + r, CHUNK), slice(None))
                    acc_ref[where] += jnp.where(from_same, same, before)

    def advance(pair, carry):
        first = 2 * pair
        second = jnp.minimum(first + 1, last_slot)
        make_exit(even, first)
        two_sided(even, fwd, inv)
        add_grads(odd, jnp.maximum(first - 1, 0))
        make_exit(odd, second)
        two_sided(odd, fwd, inv)
        make_chi(even, first, None)
        two_sided(even, inv, fwd)
        make_chi(odd, second, first + 1 < live)
        two_sided(odd, inv, fwd)
        add_grads(even, first)
        return carry

    pairs = (live + 1) // 2
    lax.fori_loop(0, pairs, advance, 0)
    add_grads(odd, jnp.minimum(2 * pairs - 1, last_slot))


def frames_call(extended, probe_modes, amplitudes, positions, live_count, tables):
    fs = probe_modes.shape[-1]
    modes = probe_modes.shape[1]
    tiled = extended.shape
    vmem = pl.BlockSpec(memory_space=pltpu.VMEM)
    smem = pl.BlockSpec(memory_space=pltpu.SMEM)
    return pl.pallas_call(
        frames_kernel,
        out_shape=(
            jax.ShapeDtypeStruct(tiled, jnp.float32),
            jax.ShapeDtypeStruct((probe_modes.size // LANES, LANES), jnp.float32),
        ),
        in_specs=[smem, smem, vmem, vmem, vmem, vmem, vmem],
        out_specs=(vmem, vmem),
        scratch_shapes=[
            pltpu.VMEM((2 * fs, 2 * fs), jnp.bfloat16),
            pltpu.VMEM((2 * fs, 2 * fs), jnp.bfloat16),
        ]
        + 2
        * [
            pltpu.VMEM((2 * fs, modes * fs), jnp.bfloat16),
            pltpu.VMEM((modes * fs, 2 * fs), jnp.bfloat16),
            pltpu.VMEM((modes * fs, 2 * fs), jnp.float32),
            pltpu.VMEM((2, fs, fs), jnp.float32),
        ],
        compiler_params=pltpu.CompilerParams(vmem_limit_bytes=26 * 1024 * 1024),
        name="frames",
    )(live_count.reshape(1), positions, extended, probe_modes, amplitudes, *tables)


def shards(object_field, probe_modes, measured_amp, scan_positions, frame_counts):
    slot_count = measured_amp.shape[2]
    extended = halo_call(object_field)
    acc, probe_flat = frames_call(
        extended,
        probe_modes,
        measured_amp[0, 0],
        scan_positions[0, 0],
        frame_counts[0, 0],
        fourier_tables(probe_modes.shape[-1]),
    )
    norm_scale = 1.0 / math.sqrt(lax.axis_size("row") * lax.axis_size("col") * slot_count)
    return reduce_call(acc, probe_flat, object_field.shape, probe_modes.shape, norm_scale)


def solution(mesh):
    in_specs = (
        P(None, "row", "col"),
        P(),
        P("row", "col", None, None, None),
        P("row", "col", None, None),
        P("row", "col"),
    )
    out_specs = (P(None, "row", "col"), P())
    return jax.shard_map(shards, mesh=mesh, in_specs=in_specs, out_specs=out_specs, check_vma=False)
```
